256 devices in a mesh: col: 8 (over z), bulk: 32 (over y, x, core).
Axes of the slice: x: 4, y: 4, z: 8, core: 2. Of those that a mesh axis runs over, the one named last changes fastest.
Arguments:
- block_input_field: bfloat16 [96, 4, 64, 1024], P(None, None, 'bulk', 'col'), may hold values from -128 to 128
- upstream_derivative: bfloat16 [96, 4, 64, 1024], P(None, None, 'bulk', 'col'), may hold values from -8 to 8
- pointwise_mixing_matrix: bfloat16 [288, 96], replicated, may hold values from -0.625 to 0.625
- per_channel_kernel: float32 [288, 27], replicated, may hold values from -1.25 to 1.25
- sharpness_per_group: float32 [2], replicated, may hold values from 0.5 to 4
Outputs:
- block_input_derivative: bfloat16 [96, 4, 64, 1024], P(None, None, 'bulk', 'col')
- pointwise_mixing_derivative: float32 [288, 96], replicated
- per_channel_kernel_derivative: float32 [288, 27], replicated
- sharpness_derivative: float32 [2], replicated
The draws below stay inside these ranges and needn't reach their ends.
All inputs are finite; a program needn't handle non-finite values.
Results may differ from the reference program's by a relative error of at most 0.00165.
The reference program's roundings to bfloat16 on the way (of `field`, `mixed`, `coupling`, `mixed_grad` and `field_grad`) count: a program that leaves them out, or rounds other values in their place, can miss the bound.
Values may be sent and summed in bfloat16 or wider, within the bound.
A program may use at most 64 MiB of HBM per device.

```python
import math
import jax
import jax.numpy as jnp
from jax import lax

C = 96
FOCUS_GROUPS = 2
Z = 4
HEAD_DIM = 48
NX = 1024
NY = 64
VOXELS = 262144


def box_along(values, axis):
    widths = [(0, 0)] * values.ndim
    widths[axis] = (1, 1)
    padded = jnp.pad(values, widths)
    length = values.shape[axis]
    lower = lax_slice(padded, axis, 0, length)
    middle = lax_slice(padded, axis, 1, length)
    upper = lax_slice(padded, axis, 2, length)
    return lower + middle + upper


def lax_slice(values, axis, start, length):
    index = [slice(None)] * values.ndim
    index[axis] = slice(start, start + length)
    return values[tuple(index)]


def common_fields(key):
    key_base = jax.random.fold_in(key, 101)
    key_vox = jax.random.fold_in(key, 102)
    key_chan = jax.random.fold_in(key, 103)
    pos_y = jnp.arange(NY, dtype=jnp.float32) / max(NY - 1, 1)
    pos_x = jnp.arange(NX, dtype=jnp.float32) / max(NX - 1, 1)
    ramp = jnp.sqrt((1.0 + 2.0 * pos_y)[:, None] * (1.0 + 2.0 * pos_x)[None, :])
    vox_scale = jnp.exp(jax.random.uniform(key_vox, (Z, NY, NX), jnp.float32, math.log(0.316), math.log(3.16)))
    chan_scale = jnp.exp(jax.random.uniform(key_chan, (C,), jnp.float32, math.log(0.316), math.log(3.16)))
    raw = jnp.clip(jax.random.normal(key_base, (C, Z, NY, NX), jnp.float32), -4.0, 4.0)
    smooth = box_along(box_along(box_along(raw, 1), 2), 3) * (1.0 / math.sqrt(27.0))
    return (smooth, chan_scale, vox_scale, ramp)


def draw_block_input_field(key, part):
    smooth, chan_scale, vox_scale, ramp = common_fields(key)
    values = smooth * chan_scale[:, None, None, None] * vox_scale[None] * ramp[None, None]
    return jnp.clip(values, -128.0, 128.0).astype(jnp.bfloat16)


def draw_upstream_derivative(key, part):
    smooth, chan_scale, vox_scale, ramp = common_fields(key)
    key_noise = jax.random.fold_in(key, 201)
    noise = jnp.clip(jax.random.normal(key_noise, (C, Z, NY, NX), jnp.float32), -4.0, 4.0)
    values = 0.8 * smooth + 0.6 * noise
    return jnp.clip(values, -8.0, 8.0).astype(jnp.bfloat16)


def gaussian(key, dims, spread, bound, kind=jnp.bfloat16):
    drawn = jax.random.normal(key, dims, jnp.float32) * spread
    return jnp.minimum(jnp.maximum(drawn, -bound), bound).astype(kind)


def setup_inputs(seed: int = 0) -> dict:
    key_of = jax.random.split(jax.random.key(seed), 6)
    block_input_field = draw_block_input_field(jax.random.fold_in(key_of[5], 71), 0)
    upstream_derivative = draw_upstream_derivative(jax.random.fold_in(key_of[5], 71), 0)
    pointwise_mixing_matrix = gaussian(key_of[2], (3 * C, C), C ** -0.5, 0.625)
    per_channel_kernel = gaussian(key_of[3], (3 * C, 27), 27 ** -0.5, 1.25, jnp.float32)
    sharpness_per_group = jnp.clip(jnp.exp(jax.random.uniform(key_of[4], (FOCUS_GROUPS,), jnp.float32, math.log(0.5), math.log(4.0))), 0.5, 4.0)
    return {"block_input_field": block_input_field, "upstream_derivative": upstream_derivative, "pointwise_mixing_matrix": pointwise_mixing_matrix, "per_channel_kernel": per_channel_kernel, "sharpness_per_group": sharpness_per_group}


def depth_apply(padded, weights, array_shape, flip):
    depth_z, rows_y, cols_x = array_shape
    total = jnp.zeros((padded.shape[0], depth_z, rows_y, cols_x), jnp.float32)
    for shift_z in range(3):
        for shift_y in range(3):
            for shift_x in range(3):
                tap = 9 * shift_z + 3 * shift_y + shift_x
                if flip:
                    start_z, start_y, start_x = (2 - shift_z, 2 - shift_y, 2 - shift_x)
                else:
                    start_z, start_y, start_x = (shift_z, shift_y, shift_x)
                window = padded[:, start_z:start_z + depth_z, start_y:start_y + rows_y, start_x:start_x + cols_x]
                total = total + weights[:, tap][:, None, None, None] * window.astype(jnp.float32)
    return total

def depth_grad(padded, grads, array_shape):
    depth_z, rows_y, cols_x = array_shape
    grads_f = grads.astype(jnp.float32)
    columns = []
    for shift_z in range(3):
        for shift_y in range(3):
            for shift_x in range(3):
                window = padded[:, shift_z:shift_z + depth_z, shift_y:shift_y + rows_y, shift_x:shift_x + cols_x]
                columns.append(lax.optimization_barrier(jnp.sum(grads_f * window.astype(jnp.float32), axis=(1, 2, 3))))
    return jnp.stack(columns, axis=1)

def pad_all(field):
    return jnp.pad(field, ((0, 0), (1, 1), (1, 1), (1, 1)))

def reference(block_input_field, upstream_derivative, pointwise_mixing_matrix, per_channel_kernel, sharpness_per_group):
    array_shape = block_input_field.shape[1:]
    flat_source = block_input_field.reshape(C, -1)
    multiplier_value = 1.0 / jnp.sqrt(jnp.float32(VOXELS))
    source_total = jnp.zeros((C, flat_source.shape[1]), jnp.float32)
    weight_rows = {}
    depth_rows = {}
    sharpness_derivative_entries = []
    contract = (((1,), (1,)), ((), ()))
    for group_index in range(FOCUS_GROUPS):
        starts = [group_index * HEAD_DIM, C + group_index * HEAD_DIM, 2 * C + group_index * HEAD_DIM]
        paddeds = []
        mixeds = []
        for start in starts:
            field = jnp.dot(pointwise_mixing_matrix[start:start + HEAD_DIM], flat_source, preferred_element_type=jnp.float32)
            field = field.astype(jnp.bfloat16).reshape((HEAD_DIM,) + array_shape)
            padded = pad_all(field)
            mixed = depth_apply(padded, per_channel_kernel[start:start + HEAD_DIM], array_shape, False).astype(jnp.bfloat16)
            paddeds.append(padded)
            mixeds.append(mixed.reshape(HEAD_DIM, -1))
        query, keys, values = mixeds
        grads_block = upstream_derivative[group_index * HEAD_DIM:(group_index + 1) * HEAD_DIM].reshape(HEAD_DIM, -1)
        sq_query = lax.optimization_barrier(jnp.sum(jnp.square(query.astype(jnp.float32)), axis=1))
        sq_keys = lax.optimization_barrier(jnp.sum(jnp.square(keys.astype(jnp.float32)), axis=1))
        gram = lax.dot_general(query, keys, contract, preferred_element_type=jnp.float32)
        value_grad = lax.dot_general(grads_block, values, contract, preferred_element_type=jnp.float32)
        inv_query = 1.0 / jnp.sqrt(sq_query + 1e-06)
        inv_keys = 1.0 / jnp.sqrt(sq_keys + 1e-06)
        normalized_similarities = gram * inv_query[:, None] * inv_keys[None, :]
        softmax_numerators = jnp.exp(sharpness_per_group[group_index] * normalized_similarities)
        attention = softmax_numerators / lax.optimization_barrier(jnp.sum(softmax_numerators, axis=1, keepdims=True))
        logit_derivative = attention * (value_grad - lax.optimization_barrier(jnp.sum(attention * value_grad, axis=1, keepdims=True)))
        sharpness_derivative_entries.append(jnp.sum(logit_derivative * normalized_similarities) * multiplier_value)
        similarity_derivative = sharpness_per_group[group_index] * logit_derivative
        diag_query = lax.optimization_barrier(jnp.sum(similarity_derivative * normalized_similarities, axis=1))
        diag_keys = lax.optimization_barrier(jnp.sum(similarity_derivative * normalized_similarities, axis=0))
        coupling = (inv_query[:, None] * similarity_derivative * inv_keys[None, :]).astype(jnp.bfloat16)
        grad_query = jnp.dot(coupling, keys, preferred_element_type=jnp.float32)
        grad_query = grad_query - (inv_query * inv_query * diag_query)[:, None] * query.astype(jnp.float32)
        grad_keys = jnp.dot(coupling.T, query, preferred_element_type=jnp.float32)
        grad_keys = grad_keys - (inv_keys * inv_keys * diag_keys)[:, None] * keys.astype(jnp.float32)
        grad_values = jnp.dot(attention.astype(jnp.bfloat16).T, grads_block, preferred_element_type=jnp.float32)
        grad_list = [grad_query, grad_keys, grad_values]
        for kind in range(3):
            start = starts[kind]
            mixed_grad = grad_list[kind].astype(jnp.bfloat16).reshape((HEAD_DIM,) + array_shape)
            field_grad = depth_apply(pad_all(mixed_grad), per_channel_kernel[start:start + HEAD_DIM], array_shape, True)
            field_grad = field_grad.astype(jnp.bfloat16).reshape(HEAD_DIM, -1)
            depth_rows[start] = depth_grad(paddeds[kind], mixed_grad, array_shape) * multiplier_value
            weight_rows[start] = lax.dot_general(field_grad, flat_source, contract, preferred_element_type=jnp.float32) * multiplier_value
            source_total = source_total + lax.dot_general(pointwise_mixing_matrix[start:start + HEAD_DIM], field_grad, (((0,), (0,)), ((), ())), preferred_element_type=jnp.float32)
    order = sorted(weight_rows.keys())
    pointwise_mixing_derivative = jnp.concatenate([weight_rows[k] for k in order], axis=0)
    per_channel_kernel_derivative = jnp.concatenate([depth_rows[k] for k in order], axis=0)
    block_input_derivative = source_total.astype(jnp.bfloat16).reshape(block_input_field.shape)
    sharpness_derivative = jnp.stack(sharpness_derivative_entries)
    return (block_input_derivative, pointwise_mixing_derivative, per_channel_kernel_derivative, sharpness_derivative)
```

```python
import functools
import math

import jax
import jax.numpy as jnp
from jax import lax
from jax.experimental import pallas as pl
from jax.experimental.pallas import tpu as pltpu
from jax.sharding import PartitionSpec as P


MESH = pl.DeviceIdType.MESH


def ring_copy(src, dst, send, recv, target):
    return pltpu.make_async_remote_copy(
        src_ref=src, dst_ref=dst, send_sem=send, recv_sem=recv, device_id=target, device_id_type=MESH
    )


def reduce_kernel(
    n_col, n_bulk, rows, x_ref, o_ref, pack, parts, planes, whole, s_send, s_recv, z_send, z_recv, g_send, g_recv
):
    col, bulk = lax.axis_index("col"), lax.axis_index("bulk")

    def other_bulk(step):
        return lax.rem(bulk + step, n_bulk)

    def other_col(step):
        return lax.rem(col + step, n_col)

    barrier = pltpu.get_barrier_semaphore()

    def greet_bulk(step, carry):
        pl.semaphore_signal(barrier, inc=1, device_id=(col, other_bulk(step)), device_id_type=MESH)
        return carry

    def greet_col(step, carry):
        pl.semaphore_signal(barrier, inc=1, device_id=(other_col(step), bulk), device_id_type=MESH)
        return carry

    lax.fori_loop(1, n_bulk, greet_bulk, 0)
    lax.fori_loop(1, n_col, greet_col, 0)
    for i in range(n_bulk):
        pack[i] = x_ref[rows * i : rows * (i + 1), :]
    pl.semaphore_wait(barrier, n_bulk + n_col - 2)

    def scatter(step):
        peer = other_bulk(step)
        return ring_copy(pack.at[peer], parts.at[bulk], s_send.at[peer], s_recv.at[bulk], (col, peer))

    def gathered(step):
        peer = other_bulk(step)
        return ring_copy(pack.at[peer], parts.at[peer], s_send.at[peer], s_recv.at[peer], (col, peer))

    def across(step):
        peer = other_col(step)
        return ring_copy(planes.at[col], planes.at[col], z_send.at[peer], z_recv.at[col], (peer, bulk))

    def arrived(step):
        peer = other_col(step)
        return ring_copy(planes.at[peer], planes.at[peer], z_send.at[peer], z_recv.at[peer], (peer, bulk))

    def spread(step):
        peer = other_bulk(step)
        return ring_copy(whole.at[bulk], whole.at[bulk], g_send.at[peer], g_recv.at[bulk], (col, peer))

    def landed(step):
        peer = other_bulk(step)
        return ring_copy(whole.at[peer], whole.at[peer], g_send.at[peer], g_recv.at[peer], (col, peer))

    def each(count, what):
        def body(step, carry):
            what(step)
            return carry

        lax.fori_loop(1, count, body, 0)

    each(n_bulk, lambda step: scatter(step).start())
    parts[bulk] = pack[bulk]
    each(n_bulk, lambda step: gathered(step).wait_recv())
    planes[col] = jnp.sum(parts[...], axis=0)
    each(n_col, lambda step: across(step).start())
    each(n_col, lambda step: arrived(step).wait_recv())
    whole[bulk] = jnp.sum(planes[...], axis=0)
    each(n_bulk, lambda step: spread(step).start())
    each(n_bulk, lambda step: scatter(step).wait_send())
    each(n_col, lambda step: across(step).wait_send())
    each(n_bulk, lambda step: landed(step).wait_recv())
    for i in range(n_bulk):
        o_ref[rows * i : rows * (i + 1), :] = whole[i]
    each(n_bulk, lambda step: spread(step).wait_send())


def reduced(x, collective_id):
    n_col, n_bulk = lax.axis_size("col"), lax.axis_size("bulk")
    rows = x.shape[0] // n_bulk
    sems = [pltpu.SemaphoreType.DMA((n_bulk,))] * 2 + [pltpu.SemaphoreType.DMA((n_col,))] * 2
    return pl.pallas_call(
        functools.partial(reduce_kernel, n_col, n_bulk, rows),
        out_shape=jax.ShapeDtypeStruct(x.shape, jnp.float32),
        in_specs=[pl.BlockSpec(memory_space=pltpu.VMEM)],
        out_specs=pl.BlockSpec(memory_space=pltpu.VMEM),
        scratch_shapes=[
            pltpu.VMEM((n_bulk, rows, 128), jnp.float32),
            pltpu.VMEM((n_bulk, rows, 128), jnp.float32),
            pltpu.VMEM((n_col, rows, 128), jnp.float32),
            pltpu.VMEM((n_bulk, rows, 128), jnp.float32),
        ]
        + sems
        + sems[:2],
        compiler_params=pltpu.CompilerParams(collective_id=collective_id, has_side_effects=True),
    )(x)


def extended(cells, sides, width):
    for axis, dim in sides:
        count = lax.axis_size(axis)
        ends = count - 1
        head = lax.slice_in_dim(cells, 0, width, axis=dim)
        tail = lax.slice_in_dim(cells, cells.shape[dim] - width, cells.shape[dim], axis=dim)
        cells = jnp.concatenate(
            [
                lax.ppermute(tail, axis, [(i, (i + 1) % count) for i in range(ends)]),
                cells,
                lax.ppermute(head, axis, [((i + 1) % count, i) for i in range(ends)]),
            ],
            axis=dim,
        )
    return cells


def depth_apply(padded, weights, array_shape, flip):
    depth_z, rows_y, cols_x = array_shape
    total = jnp.zeros((padded.shape[0], depth_z, rows_y, cols_x), jnp.float32)
    for shift_z in range(3):
        for shift_y in range(3):
            for shift_x in range(3):
                tap = 9 * shift_z + 3 * shift_y + shift_x
                if flip:
                    start_z, start_y, start_x = (2 - shift_z, 2 - shift_y, 2 - shift_x)
                else:
                    start_z, start_y, start_x = (shift_z, shift_y, shift_x)
                window = padded[
                    :,
                    start_z : start_z + depth_z,
                    start_y : start_y + rows_y,
                    start_x : start_x + cols_x,
                ]
                total = total + weights[:, tap][:, None, None, None] * window.astype(jnp.float32)
    return total


def depth_grad(padded, grads, array_shape):
    depth_z, rows_y, cols_x = array_shape
    grads_f = grads.astype(jnp.float32)
    columns = []
    for shift_z in range(3):
        for shift_y in range(3):
            for shift_x in range(3):
                window = padded[
                    :,
                    shift_z : shift_z + depth_z,
                    shift_y : shift_y + rows_y,
                    shift_x : shift_x + cols_x,
                ]
                columns.append(jnp.sum(grads_f * window.astype(jnp.float32), axis=(1, 2, 3)))
    return jnp.stack(columns, axis=1)


def pad_planes(field):
    return jnp.pad(field, ((0, 0), (1, 1), (0, 0), (0, 0)))


def head_grads(
    mixed_flat,
    cot_flat,
    coupling,
    attention,
    inv_query,
    inv_keys,
    diag_query,
    diag_keys,
    group_sequence,
    head_dim,
):
    channels = group_sequence * head_dim
    width = mixed_flat.shape[1]
    q_heads = mixed_flat[:channels].reshape(group_sequence, head_dim, width)
    k_heads = mixed_flat[channels : 2 * channels].reshape(group_sequence, head_dim, width)
    g_heads = cot_flat.reshape(group_sequence, head_dim, width)
    query_term = jnp.einsum("hij,hjv->hiv", coupling, k_heads, preferred_element_type=jnp.float32)
    keys_term = jnp.einsum("hij,hiv->hjv", coupling, q_heads, preferred_element_type=jnp.float32)
    grad_query = query_term - (inv_query * inv_query * diag_query)[:, :, None] * q_heads.astype(
        jnp.float32
    )
    grad_keys = keys_term - (inv_keys * inv_keys * diag_keys)[:, :, None] * k_heads.astype(
        jnp.float32
    )
    grad_values = jnp.einsum(
        "hij,hiv->hjv", attention.astype(jnp.bfloat16), g_heads, preferred_element_type=jnp.float32
    )
    return jnp.concatenate(
        [
            grad_query.reshape(channels, width),
            grad_keys.reshape(channels, width),
            grad_values.reshape(channels, width),
        ],
        axis=0,
    )


def local(
    block_input_field,
    upstream_derivative,
    pointwise_mixing_matrix,
    per_channel_kernel,
    sharpness_per_group,
):
    channels = block_input_field.shape[0]
    group_sequence = sharpness_per_group.shape[0]
    head_dim = channels // group_sequence
    array_shape = block_input_field.shape[1:]
    depth_z, rows_y, cols_x = array_shape
    count = depth_z * rows_y * cols_x
    voxels = count * lax.axis_size("col") * lax.axis_size("bulk")
    multiplier_value = 1.0 / math.sqrt(voxels)
    flat_source = block_input_field.reshape(channels, count)
    extra = 1
    fields = jnp.dot(pointwise_mixing_matrix, flat_source, preferred_element_type=jnp.float32)
    fields = fields.astype(jnp.bfloat16).reshape((3 * channels,) + array_shape)
    border = extended(fields, (("col", 3), ("bulk", 2)), extra)
    ext_shape = (depth_z, rows_y + 2 * extra - 2, cols_x + 2 * extra - 2)
    mixed_ext = depth_apply(pad_planes(border), per_channel_kernel, ext_shape, False).astype(
        jnp.bfloat16
    )
    padded_field = pad_planes(border)
    flat_mixed = mixed_ext.reshape(3 * channels, count)
    query = flat_mixed[:channels]
    keys_block = flat_mixed[channels : 2 * channels]
    values = flat_mixed[2 * channels :]
    q_heads = query.reshape(group_sequence, head_dim, count)
    k_heads = keys_block.reshape(group_sequence, head_dim, count)
    v_heads = values.reshape(group_sequence, head_dim, count)
    g_heads = upstream_derivative.reshape(group_sequence, head_dim, count)
    sq_query = jnp.sum(jnp.square(query.astype(jnp.float32)), axis=1)
    sq_keys = jnp.sum(jnp.square(keys_block.astype(jnp.float32)), axis=1)
    gram_local = jnp.einsum("hiv,hjv->hij", q_heads, k_heads, preferred_element_type=jnp.float32)
    value_local = jnp.einsum("hiv,hjv->hij", g_heads, v_heads, preferred_element_type=jnp.float32)
    first = jnp.concatenate(
        [
            gram_local.reshape(channels, head_dim),
            value_local.reshape(channels, head_dim),
            sq_query[:, None],
            sq_keys[:, None],
            jnp.zeros((channels, 126 - 2 * head_dim), jnp.float32),
        ],
        axis=1,
    )
    first = reduced(first, 0)
    gram = first[:, :head_dim].reshape(gram_local.shape)
    value_grad = first[:, head_dim : 2 * head_dim].reshape(gram_local.shape)
    sq_query = first[:, 2 * head_dim]
    sq_keys = first[:, 2 * head_dim + 1]
    inv_query = (1.0 / jnp.sqrt(sq_query + 1e-06)).reshape(group_sequence, head_dim)
    inv_keys = (1.0 / jnp.sqrt(sq_keys + 1e-06)).reshape(group_sequence, head_dim)
    normalized_similarities = gram * inv_query[:, :, None] * inv_keys[:, None, :]
    softmax_numerators = jnp.exp(sharpness_per_group[:, None, None] * normalized_similarities)
    attention = softmax_numerators / jnp.sum(softmax_numerators, axis=2, keepdims=True)
    logit_derivative = attention * (
        value_grad - jnp.sum(attention * value_grad, axis=2, keepdims=True)
    )
    sharpness_derivative = (
        jnp.sum(logit_derivative * normalized_similarities, axis=(1, 2)) * multiplier_value
    )
    similarity_derivative = sharpness_per_group[:, None, None] * logit_derivative
    diag_query = jnp.sum(similarity_derivative * normalized_similarities, axis=2)
    diag_keys = jnp.sum(similarity_derivative * normalized_similarities, axis=1)
    coupling = (inv_query[:, :, None] * similarity_derivative * inv_keys[:, None, :]).astype(
        jnp.bfloat16
    )
    grads_flat = head_grads(
        flat_mixed,
        upstream_derivative.reshape(channels, count),
        coupling,
        attention,
        inv_query,
        inv_keys,
        diag_query,
        diag_keys,
        group_sequence,
        head_dim,
    )
    mixed_grad = grads_flat.astype(jnp.bfloat16).reshape((3 * channels,) + array_shape)
    grad_border = extended(mixed_grad, (("col", 3), ("bulk", 2)), 1)
    field_grad = depth_apply(pad_planes(grad_border), per_channel_kernel, array_shape, True).astype(
        jnp.bfloat16
    )
    depth_local = depth_grad(padded_field, mixed_grad, array_shape)
    flat_grad = field_grad.reshape(3 * channels, count)
    weight_local = lax.dot_general(
        flat_grad, flat_source, (((1,), (1,)), ((), ())), preferred_element_type=jnp.float32
    )
    source_gradient_part = lax.dot_general(
        pointwise_mixing_matrix,
        flat_grad,
        (((0,), (0,)), ((), ())),
        preferred_element_type=jnp.float32,
    )
    source_gradient_part = source_gradient_part.astype(jnp.bfloat16).reshape(
        block_input_field.shape
    )
    second = jnp.concatenate(
        [weight_local, depth_local, jnp.zeros((3 * channels, 5), jnp.float32)], axis=1
    )
    second = reduced(second, 1)
    weight_grand_total = second[:, :channels]
    depthwise_total = second[:, channels : channels + 27]
    return (
        source_gradient_part,
        weight_grand_total * multiplier_value,
        depthwise_total * multiplier_value,
        sharpness_derivative,
    )


def solution(mesh):
    return jax.shard_map(
        local,
        mesh=mesh,
        in_specs=(P(None, None, "bulk", "col"), P(None, None, "bulk", "col"), P(), P(), P()),
        out_specs=(P(None, None, "bulk", "col"), P(), P(), P()),
        check_vma=False,
    )
```

```python
import functools
import math

import jax
import jax.numpy as jnp
import numpy as np
from jax import lax
from jax.experimental import pallas as pl
from jax.experimental.pallas import tpu as pltpu
from jax.sharding import PartitionSpec as P

MESH = pl.DeviceIdType.MESH
F32 = jnp.float32
BF16 = jnp.bfloat16
C = 96
HEAD = 48
C3 = 3 * C
LANES = 128
CHUNK = 32
EDGE_COLUMNS = (0, 1, LANES - 2, LANES - 1)
NEIGHBOURS = [(a, b) for a in (-1, 0, 1) for b in (-1, 0, 1)]


def slot_of(a, b):
    return 3 * (a + 1) + b + 1


def edge_index(z, y):
    return (z + 1) * 6 + y + 2


def edge_tables():
    place = np.zeros((3, LANES, 9 * 32), np.float32)
    flags = np.zeros((8, LANES), np.float32)
    for (a, b) in NEIGHBOURS:
        for s, column in enumerate(EDGE_COLUMNS):
            x = LANES * a + column
            for y in range(2):
                for z in range(4):
                    k = slot_of(a, b) * 32 + s * 8 + y * 4 + z
                    index = 2 * edge_index(z, 2 * b + y)
                    for c in (-1, 0, 1):
                        if x == -1 + c:
                            place[c + 1, index + 1, k] = 1.0
                        if x == LANES + c:
                            place[c + 1, index, k] = 1.0
    for z in range(4):
        for y in range(-1, 3):
            for left in range(2):
                lane = 2 * edge_index(z, y) + left
                flags[0, lane] = 1.0
                flags[1, lane] = left
                flags[2, lane] = 1 - left
                flags[3, lane] = y == -1
                flags[4, lane] = y == 2
    return place.reshape(3 * LANES, 9 * 32), flags


def dot_nt(a, b):
    return lax.dot_general(a, b, (((1,), (1,)), ((), ())), preferred_element_type=F32)


def dot_tn(a, b):
    return lax.dot_general(a, b, (((0,), (0,)), ((), ())), preferred_element_type=F32)


def dot(a, b):
    return jnp.dot(a, b, preferred_element_type=F32)


def iota(shape, dim):
    return lax.broadcasted_iota(jnp.int32, shape, dim)


def rounded(v):
    return v.astype(BF16).astype(F32)


def remote(src, dst, send, recv, target):
    return pltpu.make_async_remote_copy(
        src_ref=src, dst_ref=dst, send_sem=send, recv_sem=recv, device_id=target, device_id_type=MESH
    )


def each(count, what):
    def body(step, carry):
        what(step)
        return carry

    lax.fori_loop(1, count, body, 0)


class Reduction:
    def __init__(self, sizes, place, pack, parts, planes, whole, sems):
        self.n_col, self.n_bulk = sizes
        self.col, self.bulk = place
        self.pack, self.parts, self.planes, self.whole = pack, parts, planes, whole
        self.s_send, self.s_recv, self.z_send, self.z_recv, self.g_send, self.g_recv = sems

    def bulk_peer(self, step):
        return lax.rem(self.bulk + step, self.n_bulk)

    def col_peer(self, step):
        return lax.rem(self.col + step, self.n_col)

    def scatter(self, step, incoming=False):
        peer = self.bulk_peer(step)
        slot = peer if incoming else self.bulk
        return remote(
            self.pack.at[peer], self.parts.at[slot], self.s_send.at[peer], self.s_recv.at[slot], (self.col, peer)
        )

    def across(self, step, incoming=False):
        peer = self.col_peer(step)
        slot = peer if incoming else self.col
        return remote(
            self.planes.at[slot], self.planes.at[slot], self.z_send.at[peer], self.z_recv.at[slot], (peer, self.bulk)
        )

    def spread(self, step, incoming=False):
        peer = self.bulk_peer(step)
        slot = peer if incoming else self.bulk
        return remote(
            self.whole.at[slot], self.whole.at[slot], self.g_send.at[peer], self.g_recv.at[slot], (self.col, peer)
        )

    def start(self):
        each(self.n_bulk, lambda step: self.scatter(step).start())
        self.parts[self.bulk] = self.pack[self.bulk]

    def middle(self):
        each(self.n_bulk, lambda step: self.scatter(step, True).wait_recv())
        self.planes[self.col] = jnp.sum(self.parts[...], axis=0)
        each(self.n_col, lambda step: self.across(step).start())

    def final(self):
        each(self.n_col, lambda step: self.across(step, True).wait_recv())
        self.whole[self.bulk] = jnp.sum(self.planes[...], axis=0)
        each(self.n_bulk, lambda step: self.spread(step).start())

    def finish(self):
        each(self.n_bulk, lambda step: self.spread(step, True).wait_recv())

    def drain(self):
        each(self.n_bulk, lambda step: self.scatter(step).wait_send())
        each(self.n_col, lambda step: self.across(step).wait_send())
        each(self.n_bulk, lambda step: self.spread(step).wait_send())


def conv(source, y0, weights, flip, sink):
    def body(j, carry):
        rows = pl.ds(pl.multiple_of(j * CHUNK, CHUNK), CHUNK)
        total = [None] * 4
        for b in range(3):
            for c in range(3):
                cells = [source[c, y0 + b, z, rows, :] for z in range(4)]
                for a in range(3):
                    tap = 9 * a + 3 * b + c
                    weight = weights[26 - tap if flip else tap, rows, :]
                    for z in range(4):
                        if 0 <= z + a - 1 < 4:
                            term = weight * cells[z + a - 1]
                            total[z] = term if total[z] is None else total[z] + term
        for z in range(4):
            sink(z, rows, total[z])
        return carry

    lax.fori_loop(0, C3 // CHUNK, body, 0)


def kernel(
    sizes,
    scale,
    x_ref,
    g_ref,
    w_ref,
    k_ref,
    sharp_ref,
    place_ref,
    flags_ref,
    dx_ref,
    pd_ref,
    kd_ref,
    sd_ref,
    xh,
    gh,
    messages,
    arrived,
    edge_t,
    edge_x,
    edge_g,
    taps_t,
    taps_c,
    weights,
    field,
    field_edge,
    mixed,
    mixed_edge,
    grads,
    grads_edge,
    field_grad,
    turn,
    couple,
    coef,
    pay1,
    pay2,
    pack1,
    parts1,
    planes1,
    whole1,
    pack2,
    parts2,
    planes2,
    whole2,
    row_send,
    row_recv,
    edge_send,
    edge_recv,
    *sems,
):
    n_col, n_bulk = sizes
    col, bulk = lax.axis_index("col"), lax.axis_index("bulk")
    first = Reduction(sizes, (col, bulk), pack1, parts1, planes1, whole1, sems[:6])
    second = Reduction(sizes, (col, bulk), pack2, parts2, planes2, whole2, sems[6:])
    low, high = bulk > 0, bulk < n_bulk - 1

    xh[...] = jnp.zeros_like(xh)
    gh[...] = jnp.zeros_like(gh)
    arrived[...] = jnp.zeros_like(arrived)
    barrier = pltpu.get_barrier_semaphore()

    def greet(target):
        pl.semaphore_signal(barrier, inc=1, device_id=target, device_id_type=MESH)

    each(n_bulk, lambda step: greet((col, lax.rem(bulk + step, n_bulk))))
    each(n_col, lambda step: greet((lax.rem(col + step, n_col), bulk)))
    for a in (1, n_col - 1):
        for b in (1, n_bulk - 1):
            greet((lax.rem(col + a, n_col), lax.rem(bulk + b, n_bulk)))

    row32, lane32 = iota((32, LANES), 0), iota((32, LANES), 1)
    for k, source in enumerate((x_ref, g_ref)):
        total = jnp.zeros((32, C), F32)
        for y in range(2):
            for z in range(4):
                pick = jnp.zeros((32, LANES), jnp.bool_)
                for s, column in enumerate(EDGE_COLUMNS):
                    pick = pick | ((row32 == s * 8 + y * 4 + z) & (lane32 == column))
                total = total + dot_nt(jnp.where(pick, 1.0, 0.0).astype(BF16), source[y, z])
        messages[k] = jnp.zeros((32, LANES), BF16)
        messages[k, :, 0:C] = total.astype(BF16)

    taps_t[...] = jnp.zeros_like(taps_t)
    taps_t[0:27, 0:C3] = k_ref[...]
    for j in range(3):
        taps_c[LANES * j : LANES * (j + 1), :] = taps_t[:, LANES * j : LANES * (j + 1)].T
    for t in range(27):
        weights[t] = jnp.broadcast_to(taps_c[0:C3, t : t + 1], (C3, LANES))

    pl.semaphore_wait(barrier, n_bulk + n_col - 2 + 4)

    def row_copy(k, down):
        y = 1 if down == (k != 1) else 0
        if k == 2:
            source, target = g_ref.at[y], gh.at[0 if down else 1]
        else:
            source, target = x_ref.at[y], xh.at[(1, 0)[k] if down else (2, 3)[k]]
        sem = 2 * k + (1 if down else 0)
        return remote(source, target, row_send.at[sem], row_recv.at[sem], (col, lax.rem(bulk + (1 if down else n_bulk - 1), n_bulk)))

    def edge_copy(a, b):
        slot = slot_of(-a, -b)
        target = (lax.rem(col + a + n_col, n_col), lax.rem(bulk + b + n_bulk, n_bulk))
        return remote(messages, arrived.at[slot], edge_send.at[slot], edge_recv.at[slot], target)

    def inside(a, b):
        return (col + a >= 0) & (col + a < n_col) & (bulk + b >= 0) & (bulk + b < n_bulk)

    for (a, b) in NEIGHBOURS:
        if (a, b) != (0, 0):
            pl.when(inside(a, b))(lambda a=a, b=b: edge_copy(a, b).start())
    for k in range(3):
        pl.when(high)(lambda k=k: row_copy(k, True).start())
        pl.when(low)(lambda k=k: row_copy(k, False).start())
    arrived[slot_of(0, 0)] = messages[...]

    def wait_row(k):
        pl.when(low)(lambda: row_copy(k, True).wait_recv())
        pl.when(high)(lambda: row_copy(k, False).wait_recv())

    for (a, b) in NEIGHBOURS:
        if (a, b) != (0, 0):
            pl.when(inside(a, b))(lambda a=a, b=b: edge_copy(-a, -b).wait_recv())

    for c in range(3):
        edge_t[c] = dot(
            place_ref[LANES * c : LANES * (c + 1), :], arrived[:, 0].reshape(9 * 32, LANES)
        ).astype(BF16)
    edge_t[3] = dot(place_ref[LANES : 2 * LANES, :], arrived[:, 1].reshape(9 * 32, LANES)).astype(BF16)
    eye = jnp.where(iota((LANES, LANES), 0) == iota((LANES, LANES), 1), 1.0, 0.0).astype(BF16)
    edge_x[...] = dot_nt(eye, edge_t[1])
    edge_g[...] = dot_nt(eye, edge_t[3]).astype(BF16)
    for c in range(3):
        field_edge[c] = rounded(dot_nt(w_ref[...], edge_t[c, :, 0:C]))

    def turned(values, z, y):
        return pltpu.roll(values, LANES - 13 - 2 * (y + 2) - 12 * z, 1)

    def shifted(values, edge):
        lane = iota(values.shape, 1)
        before = jnp.where(lane == 0, edge, pltpu.roll(values, 1, 1))
        after = jnp.where(lane == LANES - 1, edge, pltpu.roll(values, LANES - 1, 1))
        return before, after

    def input_row(y):
        return x_ref.at[y] if y in (0, 1) else xh.at[{-2: 0, -1: 1, 2: 2, 3: 3}[y]]

    def make_field(ys):
        def body(z, carry):
            for y in ys:
                plane = input_row(y)[z]
                before, after = shifted(plane.astype(F32), turned(edge_x[0:C, :], z, y))
                cells = jnp.concatenate([before.astype(BF16), plane, after.astype(BF16)], axis=1)
                made = rounded(dot(w_ref[...], cells))
                for c in range(3):
                    field[c, y + 2, z] = made[:, LANES * c : LANES * (c + 1)]
            return carry

        lax.fori_loop(0, 4, body, 0)

    def make_mixed(y):
        def sink(z, rows, value):
            mixed[y + 1, z, rows, :] = value.astype(BF16)

        conv(field, y + 1, weights, False, sink)

    make_field((0, 1))
    wait_row(0)
    make_field((-1, 2))
    make_mixed(0)
    make_mixed(1)

    row, lane = iota((C, LANES), 0), iota((C, LANES), 1)
    upper = row < HEAD
    gram = jnp.zeros((C, LANES), F32)
    value = jnp.zeros((C, LANES), F32)
    square_q = jnp.zeros((C, LANES), F32)
    square_k = jnp.zeros((C, LANES), F32)
    for y in range(2):
        for z in range(4):
            q, k = mixed[y + 1, z, 0:C, :], mixed[y + 1, z, C : 2 * C, :]
            gram = gram + dot_nt(q, mixed[y + 1, z, C : C + LANES, :])
            value = value + dot_nt(g_ref[y, z], mixed[y + 1, z, C3 - LANES : C3, :])
            square_q = square_q + jnp.square(q.astype(F32))
            square_k = square_k + jnp.square(k.astype(F32))
    gram = jnp.where(upper, gram, pltpu.roll(gram, LANES - HEAD, 1))
    value = jnp.where(upper, pltpu.roll(value, 16, 1), pltpu.roll(value, LANES - 32, 1))
    sum_q = jnp.sum(square_q, axis=1, keepdims=True)
    sum_k = jnp.sum(square_k, axis=1, keepdims=True)
    pay1[...] = jnp.where(
        lane < HEAD,
        gram,
        jnp.where(lane < 2 * HEAD, value, jnp.where(lane == C, sum_q, jnp.where(lane == C + 1, sum_k, 0.0))),
    )
    rows1 = C // n_bulk
    for i in range(n_bulk):
        pack1[i] = pay1[rows1 * i : rows1 * (i + 1), :]
    first.start()

    wait_row(1)
    make_field((-2, 3))
    spread_edge = []
    for a in range(3):
        for b in range(3):
            part = None
            for c in range(3):
                term = weights[9 * a + 3 * b + c] * field_edge[c]
                part = term if part is None else part + term
            step = 12 * (a - 1) + 2 * (b - 1)
            spread_edge.append(pltpu.roll(part, (LANES - step) % LANES, 1))
    mixed_edge[...] = sum(spread_edge[1:], spread_edge[0]).astype(BF16)
    make_mixed(-1)
    first.middle()
    make_mixed(2)
    wait_row(2)
    first.final()
    first.finish()

    for i in range(n_bulk):
        pay1[rows1 * i : rows1 * (i + 1), :] = whole1[i]
    sums = pay1[...]
    value = pltpu.roll(sums, LANES - HEAD, 1)
    inv_q = 1.0 / jnp.sqrt(sums[:, C : C + 1] + 1e-06)
    inv_k = 1.0 / jnp.sqrt(sums[:, C + 1 : C + 2] + 1e-06)
    inv_k0 = jnp.sum(jnp.where(row == lane, inv_k, 0.0), axis=0, keepdims=True)
    inv_k1 = jnp.sum(jnp.where(row == lane + HEAD, inv_k, 0.0), axis=0, keepdims=True)
    inv_kr = jnp.where(upper, inv_k0, inv_k1)
    inner = lane < HEAD
    sharp = jnp.where(upper, sharp_ref[0], sharp_ref[1])
    cosine = jnp.where(inner, sums * inv_q * inv_kr, 0.0)
    numerators = jnp.where(inner, jnp.exp(sharp * cosine), 0.0)
    attention = numerators / jnp.sum(numerators, axis=1, keepdims=True)
    score = attention * (value - jnp.sum(attention * value, axis=1, keepdims=True))
    by_cosine = score * cosine
    sd_ref[0] = jnp.sum(jnp.where(upper, by_cosine, 0.0)) * scale
    sd_ref[1] = jnp.sum(jnp.where(upper, 0.0, by_cosine)) * scale
    cosine_grad = sharp * score
    diagonal = cosine_grad * cosine
    diag_q = jnp.sum(diagonal, axis=1, keepdims=True)
    coupling = rounded(inv_q * cosine_grad * inv_kr)

    def blocks(v):
        return jnp.where(
            upper, jnp.where(inner, v, 0.0), jnp.where((lane >= HEAD) & (lane < C), pltpu.roll(v, HEAD, 1), 0.0)
        )

    def transposed(v):
        turn[0:C, :] = v
        turn[C:LANES, :] = jnp.zeros((LANES - C, LANES), F32)
        return turn[...].T

    coupled = blocks(coupling)
    couple[0] = coupled.astype(BF16)
    couple[1] = transposed(coupled)[0:C, :].astype(BF16)
    couple[2] = transposed(blocks(attention))[0:C, :].astype(BF16)
    diag_k = jnp.sum(transposed(blocks(diagonal)), axis=1, keepdims=True)[0:C, :]
    coef[0] = jnp.broadcast_to(inv_q * inv_q * diag_q, (C, LANES))
    coef[1] = jnp.broadcast_to(inv_k * inv_k * diag_k, (C, LANES))

    def gradients(q, k, g):
        grad_q = dot(couple[0, :, 0:C], k) - coef[0] * q.astype(F32)
        grad_k = dot(couple[1, :, 0:C], q) - coef[1] * k.astype(F32)
        return grad_q, grad_k, dot(couple[2, :, 0:C], g)

    def flag(condition):
        return jnp.where(condition, 1.0, 0.0)

    mask = (
        flags_ref[0:1, :]
        * (1.0 - flags_ref[1:2, :] * flag(col == 0))
        * (1.0 - flags_ref[2:3, :] * flag(col == n_col - 1))
        * (1.0 - flags_ref[3:4, :] * flag(bulk == 0))
        * (1.0 - flags_ref[4:5, :] * flag(bulk == n_bulk - 1))
    )
    edges = gradients(mixed_edge[0:C, :], mixed_edge[C : 2 * C, :], edge_g[0:C, :])
    for part in range(3):
        grads_edge[C * part : C * (part + 1), :] = jnp.where(mask > 0.5, rounded(edges[part]), 0.0)

    def grad_planes(z, carry):
        for y in range(-1, 3):
            g = g_ref[y, z] if y in (0, 1) else gh[0 if y == -1 else 1, z]
            made = gradients(mixed[y + 1, z, 0:C, :], mixed[y + 1, z, C : 2 * C, :], g)
            for part in range(3):
                rows = slice(C * part, C * (part + 1))
                plane = rounded(made[part])
                if y == -1:
                    plane = plane * flag(low)
                if y == 2:
                    plane = plane * flag(high)
                before, after = shifted(plane, turned(grads_edge[rows, :], z, y))
                grads[0, y + 1, z, rows, :] = before
                grads[1, y + 1, z, rows, :] = plane
                grads[2, y + 1, z, rows, :] = after
        return carry

    lax.fori_loop(0, 4, grad_planes, 0)

    for y in range(2):

        def sink(z, rows, value, y=y):
            field_grad[y, z, rows, :] = value.astype(BF16)

        conv(grads, y, weights, True, sink)

    weight = jnp.zeros((C3, C), F32)
    for y in range(2):
        for z in range(4):
            weight = weight + dot_nt(field_grad[y, z], x_ref[y, z])
    pay2[:, 0:C] = weight

    def depth(j, carry):
        rows = pl.ds(pl.multiple_of(j * CHUNK, CHUNK), CHUNK)
        lane = iota((CHUNK, LANES), 1)
        made = pay2[rows, :]
        for b in range(3):
            for c in range(3):
                for a in range(3):
                    total = None
                    for y in range(2):
                        for z in range(4):
                            if 0 <= z + a - 1 < 4:
                                term = grads[1, y + 1, z, rows, :] * field[c, y + b + 1, z + a - 1, rows, :]
                                total = term if total is None else total + term
                    tap = 9 * a + 3 * b + c
                    made = jnp.where(lane == C + tap, jnp.sum(total, axis=1, keepdims=True), made)
        pay2[rows, :] = jnp.where(lane < C + 27, made, 0.0)
        return carry

    lax.fori_loop(0, C3 // CHUNK, depth, 0)
    rows2 = C3 // n_bulk
    for i in range(n_bulk):
        pack2[i] = pay2[rows2 * i : rows2 * (i + 1), :]
    second.start()

    for y in range(2):
        for z in range(4):
            dx_ref[y, z] = dot_tn(w_ref[...], field_grad[y, z]).astype(BF16)
    for k in range(3):
        pl.when(high)(lambda k=k: row_copy(k, True).wait_send())
        pl.when(low)(lambda k=k: row_copy(k, False).wait_send())
    for (a, b) in NEIGHBOURS:
        if (a, b) != (0, 0):
            pl.when(inside(a, b))(lambda a=a, b=b: edge_copy(a, b).wait_send())
    first.drain()
    second.middle()
    second.final()
    second.finish()
    for i in range(n_bulk):
        pay2[rows2 * i : rows2 * (i + 1), :] = whole2[i]
    pd_ref[...] = pay2[:, 0:C] * scale
    kd_ref[...] = pay2[:, C : C + 27] * scale
    second.drain()


def local(x, g, w, k, sharp):
    n_col, n_bulk = lax.axis_size("col"), lax.axis_size("bulk")
    scale = 1.0 / math.sqrt(x.shape[1] * x.shape[2] * x.shape[3] * n_col * n_bulk)
    place, flags = edge_tables()
    vmem = pl.BlockSpec(memory_space=pltpu.VMEM)
    smem = pl.BlockSpec(memory_space=pltpu.SMEM)
    rows1, rows2 = C // n_bulk, C3 // n_bulk

    def reduction(rows):
        return [
            pltpu.VMEM((n_bulk, rows, LANES), F32),
            pltpu.VMEM((n_bulk, rows, LANES), F32),
            pltpu.VMEM((n_col, rows, LANES), F32),
            pltpu.VMEM((n_bulk, rows, LANES), F32),
        ]

    def dma(count):
        return pltpu.SemaphoreType.DMA((count,))

    reduction_sems = [dma(n_bulk), dma(n_bulk), dma(n_col), dma(n_col), dma(n_bulk), dma(n_bulk)]
    dx, pd, kd, sd = pl.pallas_call(
        functools.partial(kernel, (n_col, n_bulk), scale),
        out_shape=(
            jax.ShapeDtypeStruct((2, 4, C, LANES), BF16),
            jax.ShapeDtypeStruct((C3, C), F32),
            jax.ShapeDtypeStruct((C3, 27), F32),
            jax.ShapeDtypeStruct((2,), F32),
        ),
        in_specs=[vmem, vmem, vmem, vmem, smem, vmem, vmem],
        out_specs=(vmem, vmem, vmem, smem),
        scratch_shapes=[
            pltpu.VMEM((4, 4, C, LANES), BF16),
            pltpu.VMEM((2, 4, C, LANES), BF16),
            pltpu.VMEM((2, 32, LANES), BF16),
            pltpu.VMEM((9, 2, 32, LANES), BF16),
            pltpu.VMEM((4, LANES, LANES), BF16),
            pltpu.VMEM((LANES, LANES), F32),
            pltpu.VMEM((LANES, LANES), BF16),
            pltpu.VMEM((LANES, 3 * LANES), F32),
            pltpu.VMEM((3 * LANES, LANES), F32),
            pltpu.VMEM((27, C3, LANES), F32),
            pltpu.VMEM((3, 6, 4, C3, LANES), F32),
            pltpu.VMEM((3, C3, LANES), F32),
            pltpu.VMEM((4, 4, C3, LANES), BF16),
            pltpu.VMEM((C3, LANES), BF16),
            pltpu.VMEM((3, 4, 4, C3, LANES), F32),
            pltpu.VMEM((C3, LANES), F32),
            pltpu.VMEM((2, 4, C3, LANES), BF16),
            pltpu.VMEM((LANES, LANES), F32),
            pltpu.VMEM((3, C, LANES), BF16),
            pltpu.VMEM((2, C, LANES), F32),
            pltpu.VMEM((C, LANES), F32),
            pltpu.VMEM((C3, LANES), F32),
        ]
        + reduction(rows1)
        + reduction(rows2)
        + [dma(6), dma(6), dma(9), dma(9)]
        + reduction_sems
        + reduction_sems,
        compiler_params=pltpu.CompilerParams(
            collective_id=0, has_side_effects=True, vmem_limit_bytes=56 * 2**20
        ),
    )(
        jnp.transpose(x, (2, 1, 0, 3)),
        jnp.transpose(g, (2, 1, 0, 3)),
        w,
        k.T,
        sharp,
        jnp.asarray(place, BF16),
        jnp.asarray(flags),
    )
    return jnp.transpose(dx, (2, 1, 0, 3)), pd, kd, sd


def solution(mesh):
    return jax.shard_map(
        local,
        mesh=mesh,
        in_specs=(P(None, None, "bulk", "col"), P(None, None, "bulk", "col"), P(), P(), P()),
        out_specs=(P(None, None, "bulk", "col"), P(), P(), P()),
        check_vma=False,
    )
```

```python
import functools
import math

import jax
import jax.numpy as jnp
import numpy as np
from jax import lax
from jax.experimental import pallas as pl
from jax.experimental.pallas import tpu as pltpu
from jax.sharding import PartitionSpec as P

MESH = pl.DeviceIdType.MESH
F32 = jnp.float32
BF16 = jnp.bfloat16
C = 96
HEAD = 48
C3 = 3 * C
LANES = 128
CHUNK = 32
DEPTH_CHUNK = 32
EDGE_COLUMNS = (0, 1, LANES - 2, LANES - 1)
NEIGHBOURS = [(a, b) for a in (-1, 0, 1) for b in (-1, 0, 1)]


def slot_of(a, b):
    return 3 * (a + 1) + b + 1


def edge_index(z, y):
    return (z + 1) * 6 + y + 2


def edge_tables():
    place = np.zeros((3, LANES, 9 * 32), np.float32)
    flags = np.zeros((8, LANES), np.float32)
    for (a, b) in NEIGHBOURS:
        for s, column in enumerate(EDGE_COLUMNS):
            x = LANES * a + column
            for y in range(2):
                for z in range(4):
                    k = slot_of(a, b) * 32 + s * 8 + y * 4 + z
                    index = 2 * edge_index(z, 2 * b + y)
                    for c in (-1, 0, 1):
                        if x == -1 + c:
                            place[c + 1, index + 1, k] = 1.0
                        if x == LANES + c:
                            place[c + 1, index, k] = 1.0
    for z in range(4):
        for y in range(-1, 3):
            for left in range(2):
                lane = 2 * edge_index(z, y) + left
                flags[0, lane] = 1.0
                flags[1, lane] = left
                flags[2, lane] = 1 - left
                flags[3, lane] = y == -1
                flags[4, lane] = y == 2
    return place.reshape(3 * LANES, 9 * 32), flags


def dot_nt(a, b):
    return lax.dot_general(a, b, (((1,), (1,)), ((), ())), preferred_element_type=F32)


def dot_tn(a, b):
    return lax.dot_general(a, b, (((0,), (0,)), ((), ())), preferred_element_type=F32)


def dot(a, b):
    return jnp.dot(a, b, preferred_element_type=F32)


def iota(shape, dim):
    return lax.broadcasted_iota(jnp.int32, shape, dim)


def rounded(v):
    return v.astype(BF16).astype(F32)


def remote(src, dst, send, recv, target):
    return pltpu.make_async_remote_copy(
        src_ref=src, dst_ref=dst, send_sem=send, recv_sem=recv, device_id=target, device_id_type=MESH
    )


def ring_distance(step, count):
    return min(step, count - step)


def bulk_peers(bulk, n_bulk):
    if n_bulk != 32:
        return [lax.rem(bulk + step, n_bulk) for step in range(1, n_bulk)]
    ys = [lax.rem(bulk // 8 + d, 4) * 8 for d in range(4)]
    xs = [lax.rem(lax.rem(bulk // 2, 4) + d, 4) * 2 for d in range(4)]
    cores = [lax.rem(bulk + d, 2) for d in range(2)]
    steps = [(y, x, c) for y in range(4) for x in range(4) for c in range(2)][1:]
    steps.sort(key=lambda t: -2 * ring_distance(t[0], 4) - 2 * ring_distance(t[1], 4) - t[2])
    return [ys[y] + xs[x] + cores[c] for y, x, c in steps]


def col_peers(col, n_col):
    steps = sorted(range(1, n_col), key=lambda d: -ring_distance(d, n_col))
    return [lax.rem(col + d, n_col) for d in steps]


class Reduction:
    def __init__(self, place, peers, pack, parts, planes, whole, sems):
        self.col, self.bulk = place
        self.in_plane, self.in_col = peers
        self.pack, self.parts, self.planes, self.whole = pack, parts, planes, whole
        self.s_send, self.s_recv, self.z_send, self.z_recv, self.g_send, self.g_recv = sems

    def scattered(self):
        rest = pl.ds(0, len(self.in_plane))
        target = (self.col, self.in_plane[0])
        return remote(self.pack.at[rest], self.parts.at[rest], self.s_send, self.s_recv, target)

    def crossed(self):
        rest = pl.ds(0, len(self.in_col))
        target = (self.in_col[0], self.bulk)
        return remote(self.planes.at[rest], self.planes.at[rest], self.z_send, self.z_recv, target)

    def gathered(self):
        rest = pl.ds(0, len(self.in_plane))
        target = (self.col, self.in_plane[0])
        return remote(self.whole.at[rest], self.whole.at[rest], self.g_send, self.g_recv, target)

    def start(self):
        for peer in self.in_plane:
            remote(
                self.pack.at[peer], self.parts.at[self.bulk], self.s_send, self.s_recv, (self.col, peer)
            ).start()
        self.parts[self.bulk] = self.pack[self.bulk]

    def middle(self):
        self.scattered().wait_recv()
        self.planes[self.col] = jnp.sum(self.parts[...], axis=0)
        mine = self.planes.at[self.col]
        for peer in self.in_col:
            remote(mine, mine, self.z_send, self.z_recv, (peer, self.bulk)).start()

    def final(self):
        self.crossed().wait_recv()
        self.whole[self.bulk] = jnp.sum(self.planes[...], axis=0)
        mine = self.whole.at[self.bulk]
        for peer in self.in_plane:
            remote(mine, mine, self.g_send, self.g_recv, (self.col, peer)).start()

    def finish(self):
        self.gathered().wait_recv()

    def drain(self):
        self.scattered().wait_send()
        self.crossed().wait_send()
        self.gathered().wait_send()


def conv(source, y0, weights, flip, sink):
    def body(j, carry):
        rows = pl.ds(pl.multiple_of(j * CHUNK, CHUNK), CHUNK)
        total = [None] * 4
        for b in range(3):
            for c in range(3):
                cells = [source[c, y0 + b, z, rows, :] for z in range(4)]
                for a in range(3):
                    tap = 9 * a + 3 * b + c
                    weight = weights[26 - tap if flip else tap, rows, :]
                    for z in range(4):
                        if 0 <= z + a - 1 < 4:
                            term = weight * cells[z + a - 1]
                            total[z] = term if total[z] is None else total[z] + term
        for z in range(4):
            sink(z, rows, total[z])
        return carry

    lax.fori_loop(0, C3 // CHUNK, body, 0)


def kernel(
    sizes,
    scale,
    x_in,
    g_in,
    w_ref,
    k_ref,
    sharp_ref,
    place_ref,
    flags_ref,
    dx_ref,
    pd_ref,
    kd_ref,
    sd_ref,
    x_ref,
    g_ref,
    xh,
    gh,
    messages,
    arrived,
    edge_t,
    edge_x,
    edge_g,
    taps_t,
    taps_c,
    weights,
    field,
    field_edge,
    mixed,
    mixed_edge,
    grads,
    grads_edge,
    field_grad,
    turn,
    couple,
    coef,
    pay1,
    pay2,
    pack1,
    parts1,
    planes1,
    whole1,
    pack2,
    parts2,
    planes2,
    whole2,
    row_send,
    row_recv,
    edge_send,
    edge_recv,
    *sems,
):
    n_col, n_bulk = sizes
    col, bulk = lax.axis_index("col"), lax.axis_index("bulk")
    peers = bulk_peers(bulk, n_bulk), col_peers(col, n_col)
    first = Reduction((col, bulk), peers, pack1, parts1, planes1, whole1, sems[:6])
    second = Reduction((col, bulk), peers, pack2, parts2, planes2, whole2, sems[6:])
    low, high = bulk > 0, bulk < n_bulk - 1

    xh[...] = jnp.zeros_like(xh)
    gh[...] = jnp.zeros_like(gh)
    arrived[...] = jnp.zeros_like(arrived)
    barrier = pltpu.get_barrier_semaphore()

    def greet(target):
        pl.semaphore_signal(barrier, inc=1, device_id=target, device_id_type=MESH)

    for a in (1, n_col - 1):
        for b in (1, n_bulk - 1):
            greet((lax.rem(col + a, n_col), lax.rem(bulk + b, n_bulk)))
    for peer in reversed(peers[1]):
        greet((peer, bulk))
    for peer in reversed(peers[0]):
        greet((col, peer))

    for source, planes in ((x_in, x_ref), (g_in, g_ref)):
        for z in range(4):
            pair = source[:, z].astype(F32)
            for y in range(2):
                planes[y, z] = pair[:, y, :].astype(BF16)
    row32, lane32 = iota((32, LANES), 0), iota((32, LANES), 1)
    for k, source in enumerate((x_ref, g_ref)):
        total = jnp.zeros((32, C), F32)
        for y in range(2):
            for z in range(4):
                pick = jnp.zeros((32, LANES), jnp.bool_)
                for s, column in enumerate(EDGE_COLUMNS):
                    pick = pick | ((row32 == s * 8 + y * 4 + z) & (lane32 == column))
                total = total + dot_nt(jnp.where(pick, 1.0, 0.0).astype(BF16), source[y, z])
        messages[k] = jnp.zeros((32, LANES), BF16)
        messages[k, :, 0:C] = total.astype(BF16)

    pl.semaphore_wait(barrier, n_bulk + n_col - 2 + 4)

    def row_copy(k, down):
        y = 1 if down == (k != 1) else 0
        if k == 2:
            source, target = g_ref.at[y], gh.at[0 if down else 1]
        else:
            source, target = x_ref.at[y], xh.at[(1, 0)[k] if down else (2, 3)[k]]
        sem = 2 * k + (1 if down else 0)
        return remote(source, target, row_send.at[sem], row_recv.at[sem], (col, lax.rem(bulk + (1 if down else n_bulk - 1), n_bulk)))

    def edge_copy(a, b):
        slot = slot_of(-a, -b)
        target = (lax.rem(col + a + n_col, n_col), lax.rem(bulk + b + n_bulk, n_bulk))
        return remote(messages, arrived.at[slot], edge_send.at[slot], edge_recv.at[slot], target)

    def inside(a, b):
        return (col + a >= 0) & (col + a < n_col) & (bulk + b >= 0) & (bulk + b < n_bulk)

    for (a, b) in NEIGHBOURS:
        if (a, b) != (0, 0):
            pl.when(inside(a, b))(lambda a=a, b=b: edge_copy(a, b).start())
    for k in range(3):
        pl.when(high)(lambda k=k: row_copy(k, True).start())
        pl.when(low)(lambda k=k: row_copy(k, False).start())
    arrived[slot_of(0, 0)] = messages[...]

    def wait_row(k):
        pl.when(low)(lambda: row_copy(k, True).wait_recv())
        pl.when(high)(lambda: row_copy(k, False).wait_recv())

    def turned(values, z, y):
        return pltpu.roll(values, LANES - 1 - 2 * edge_index(z, y), 1)

    def shifted(values, edge):
        lane = iota(values.shape, 1)
        before = jnp.where(lane == 0, edge, pltpu.roll(values, 1, 1))
        after = jnp.where(lane == LANES - 1, edge, pltpu.roll(values, LANES - 1, 1))
        return before, after

    def input_row(y):
        return x_ref.at[y] if y in (0, 1) else xh.at[{-2: 0, -1: 1, 2: 2, 3: 3}[y]]

    def make_field(ys):
        for y in ys:
            for z in range(4):
                plane = input_row(y)[z]
                wide = plane.astype(F32)
                edge = wide if y in (0, 1) else turned(edge_x[0:C, :], z, y)
                before, after = shifted(wide, edge)
                cells = jnp.concatenate([before.astype(BF16), plane, after.astype(BF16)], axis=1)
                made = rounded(dot(w_ref[...], cells))
                for c in range(3):
                    field[c, y + 2, z] = made[:, LANES * c : LANES * (c + 1)]

    def make_mixed(y):
        def sink(z, rows, value):
            mixed[y + 1, z, rows, :] = value.astype(BF16)

        conv(field, y + 1, weights, False, sink)

    taps_t[...] = jnp.zeros_like(taps_t)
    taps_t[0:27, 0:C3] = k_ref[...]
    for j in range(3):
        taps_c[LANES * j : LANES * (j + 1), :] = taps_t[:, LANES * j : LANES * (j + 1)].T
    for t in range(27):
        weights[t] = jnp.broadcast_to(taps_c[0:C3, t : t + 1], (C3, LANES))

    make_field((0, 1))
    for (a, b) in NEIGHBOURS:
        if (a, b) != (0, 0):
            pl.when(inside(a, b))(lambda a=a, b=b: edge_copy(-a, -b).wait_recv())

    def placed(c, kind):
        return dot(place_ref[LANES * c : LANES * (c + 1), :], arrived[:, kind].reshape(9 * 32, LANES)).astype(BF16)

    eye = jnp.where(iota((LANES, LANES), 0) == iota((LANES, LANES), 1), 1.0, 0.0).astype(BF16)
    edge_t[1] = placed(1, 0)
    edge_x[...] = dot_nt(eye, edge_t[1])
    field_edge[1] = rounded(dot_nt(w_ref[...], edge_t[1, :, 0:C]))
    for y in range(2):
        for z in range(4):
            edge = turned(field_edge[1], z, y)
            field[0, y + 2, z, :, 0:1] = edge[:, 0:1]
            field[2, y + 2, z, :, LANES - 1 : LANES] = edge[:, LANES - 1 : LANES]
    wait_row(0)
    make_field((-1, 2))
    make_mixed(0)
    make_mixed(1)

    row, lane = iota((C, LANES), 0), iota((C, LANES), 1)
    upper = row < HEAD
    gram = jnp.zeros((C, LANES), F32)
    value = jnp.zeros((C, LANES), F32)
    square_q = jnp.zeros((C, LANES), F32)
    square_k = jnp.zeros((C, LANES), F32)
    for y in range(2):
        for z in range(4):
            q, k = mixed[y + 1, z, 0:C, :], mixed[y + 1, z, C : 2 * C, :]
            gram = gram + dot_nt(q, mixed[y + 1, z, C : C + LANES, :])
            value = value + dot_nt(g_ref[y, z], mixed[y + 1, z, C3 - LANES : C3, :])
            square_q = square_q + jnp.square(q.astype(F32))
            square_k = square_k + jnp.square(k.astype(F32))
    gram = jnp.where(upper, gram, pltpu.roll(gram, LANES - HEAD, 1))
    value = jnp.where(upper, pltpu.roll(value, 16, 1), pltpu.roll(value, LANES - 32, 1))
    sum_q = jnp.sum(square_q, axis=1, keepdims=True)
    sum_k = jnp.sum(square_k, axis=1, keepdims=True)
    pay1[...] = jnp.where(
        lane < HEAD,
        gram,
        jnp.where(lane < 2 * HEAD, value, jnp.where(lane == C, sum_q, jnp.where(lane == C + 1, sum_k, 0.0))),
    )
    rows1 = C // n_bulk
    for i in range(n_bulk):
        pack1[i] = pay1[rows1 * i : rows1 * (i + 1), :]
    first.start()

    wait_row(1)
    make_field((-2, 3))
    for c in (0, 2):
        edge_t[c] = placed(c, 0)
        field_edge[c] = rounded(dot_nt(w_ref[...], edge_t[c, :, 0:C]))
    edge_t[3] = placed(1, 1)
    edge_g[...] = dot_nt(eye, edge_t[3]).astype(BF16)
    spread_edge = []
    for a in range(3):
        for b in range(3):
            part = None
            for c in range(3):
                term = weights[9 * a + 3 * b + c] * field_edge[c]
                part = term if part is None else part + term
            step = 12 * (a - 1) + 2 * (b - 1)
            spread_edge.append(pltpu.roll(part, (LANES - step) % LANES, 1))
    mixed_edge[...] = sum(spread_edge[1:], spread_edge[0]).astype(BF16)
    make_mixed(-1)
    first.middle()
    make_mixed(2)
    wait_row(2)
    first.final()
    first.finish()

    for i in range(n_bulk):
        pay1[rows1 * i : rows1 * (i + 1), :] = whole1[i]
    sums = pay1[...]
    value = pltpu.roll(sums, LANES - HEAD, 1)
    inv_q = 1.0 / jnp.sqrt(sums[:, C : C + 1] + 1e-06)
    inv_k = 1.0 / jnp.sqrt(sums[:, C + 1 : C + 2] + 1e-06)
    inv_k0 = jnp.sum(jnp.where(row == lane, inv_k, 0.0), axis=0, keepdims=True)
    inv_k1 = jnp.sum(jnp.where(row == lane + HEAD, inv_k, 0.0), axis=0, keepdims=True)
    inv_kr = jnp.where(upper, inv_k0, inv_k1)
    inner = lane < HEAD
    sharp = jnp.where(upper, sharp_ref[0], sharp_ref[1])
    cosine = jnp.where(inner, sums * inv_q * inv_kr, 0.0)
    numerators = jnp.where(inner, jnp.exp(sharp * cosine), 0.0)
    attention = numerators / jnp.sum(numerators, axis=1, keepdims=True)
    score = attention * (value - jnp.sum(attention * value, axis=1, keepdims=True))
    by_cosine = score * cosine
    sd_ref[0] = jnp.sum(jnp.where(upper, by_cosine, 0.0)) * scale
    sd_ref[1] = jnp.sum(jnp.where(upper, 0.0, by_cosine)) * scale
    cosine_grad = sharp * score
    diagonal = cosine_grad * cosine
    diag_q = jnp.sum(diagonal, axis=1, keepdims=True)
    coupling = rounded(inv_q * cosine_grad * inv_kr)

    def blocks(v):
        return jnp.where(
            upper, jnp.where(inner, v, 0.0), jnp.where((lane >= HEAD) & (lane < C), pltpu.roll(v, HEAD, 1), 0.0)
        )

    def transposed(v):
        turn[0:C, :] = v
        turn[C:LANES, :] = jnp.zeros((LANES - C, LANES), F32)
        return turn[...].T

    coupled = blocks(coupling)
    couple[0] = coupled.astype(BF16)
    couple[1] = transposed(coupled)[0:C, :].astype(BF16)
    couple[2] = transposed(blocks(attention))[0:C, :].astype(BF16)
    diag_k = jnp.sum(transposed(blocks(diagonal)), axis=1, keepdims=True)[0:C, :]
    coef[0] = jnp.broadcast_to(inv_q * inv_q * diag_q, (C, LANES))
    coef[1] = jnp.broadcast_to(inv_k * inv_k * diag_k, (C, LANES))

    def gradients(q, k, g):
        grad_q = dot(couple[0, :, 0:C], k) - coef[0] * q.astype(F32)
        grad_k = dot(couple[1, :, 0:C], q) - coef[1] * k.astype(F32)
        return grad_q, grad_k, dot(couple[2, :, 0:C], g)

    def flag(condition):
        return jnp.where(condition, 1.0, 0.0)

    mask = (
        flags_ref[0:1, :]
        * (1.0 - flags_ref[1:2, :] * flag(col == 0))
        * (1.0 - flags_ref[2:3, :] * flag(col == n_col - 1))
        * (1.0 - flags_ref[3:4, :] * flag(bulk == 0))
        * (1.0 - flags_ref[4:5, :] * flag(bulk == n_bulk - 1))
    )
    edges = gradients(mixed_edge[0:C, :], mixed_edge[C : 2 * C, :], edge_g[0:C, :])
    for part in range(3):
        grads_edge[C * part : C * (part + 1), :] = jnp.where(mask > 0.5, rounded(edges[part]), 0.0)

    def grad_planes(z):
        for y in range(-1, 3):
            g = g_ref[y, z] if y in (0, 1) else gh[0 if y == -1 else 1, z]
            made = gradients(mixed[y + 1, z, 0:C, :], mixed[y + 1, z, C : 2 * C, :], g)
            for part in range(3):
                rows = slice(C * part, C * (part + 1))
                plane = rounded(made[part])
                if y == -1:
                    plane = plane * flag(low)
                if y == 2:
                    plane = plane * flag(high)
                before, after = shifted(plane, turned(grads_edge[rows, :], z, y))
                grads[0, y + 1, z, rows, :] = before
                grads[1, y + 1, z, rows, :] = plane
                grads[2, y + 1, z, rows, :] = after

    for z in range(4):
        grad_planes(z)

    for y in range(2):

        def sink(z, rows, value, y=y):
            field_grad[y, z, rows, :] = value.astype(BF16)

        conv(grads, y, weights, True, sink)

    weight = jnp.zeros((C3, C), F32)
    for y in range(2):
        for z in range(4):
            weight = weight + dot_nt(field_grad[y, z], x_ref[y, z])
    pay2[:, 0:C] = weight

    def depth(j, carry):
        rows = pl.ds(pl.multiple_of(j * DEPTH_CHUNK, DEPTH_CHUNK), DEPTH_CHUNK)
        lane = iota((DEPTH_CHUNK, LANES), 1)
        made = pay2[rows, :]
        mine = [[grads[1, y + 1, z, rows, :] for z in range(4)] for y in range(2)]
        for b in range(3):
            for c in range(3):
                cells = [[field[c, y + b + 1, z, rows, :] for z in range(4)] for y in range(2)]
                for a in range(3):
                    total = None
                    for y in range(2):
                        for z in range(4):
                            if 0 <= z + a - 1 < 4:
                                term = mine[y][z] * cells[y][z + a - 1]
                                total = term if total is None else total + term
                    tap = 9 * a + 3 * b + c
                    made = jnp.where(lane == C + tap, jnp.sum(total, axis=1, keepdims=True), made)
        pay2[rows, :] = jnp.where(lane < C + 27, made, 0.0)
        return carry

    lax.fori_loop(0, C3 // DEPTH_CHUNK, depth, 0)
    rows2 = C3 // n_bulk
    for i in range(n_bulk):
        pack2[i] = pay2[rows2 * i : rows2 * (i + 1), :]
    second.start()

    for z in range(4):
        rows_y = [dot_tn(w_ref[...], field_grad[y, z]) for y in range(2)]
        dx_ref[:, z] = jnp.stack(rows_y, axis=1).astype(BF16)
    for k in range(3):
        pl.when(high)(lambda k=k: row_copy(k, True).wait_send())
        pl.when(low)(lambda k=k: row_copy(k, False).wait_send())
    for (a, b) in NEIGHBOURS:
        if (a, b) != (0, 0):
            pl.when(inside(a, b))(lambda a=a, b=b: edge_copy(a, b).wait_send())
    first.drain()
    second.middle()
    second.final()
    second.finish()
    for i in range(n_bulk):
        pay2[rows2 * i : rows2 * (i + 1), :] = whole2[i]
    pd_ref[...] = pay2[:, 0:C] * scale
    taps_c[0:C3, :] = pay2[...] * scale
    for j in range(3):
        taps_t[:, LANES * j : LANES * (j + 1)] = taps_c[LANES * j : LANES * (j + 1), :].T
    kd_ref[...] = taps_t[C : C + 27, 0:C3]
    second.drain()


def hand_out(dx_in, pd_in, kd_in, sd_in, dx_ref, pd_ref, kd_ref, sd_ref):
    dx_ref[...] = dx_in[...]
    pd_ref[...] = pd_in[...]
    kd_ref[...] = kd_in[...]
    for e in range(2):
        sd_ref[e] = sd_in[e]


def local(x, g, w, k, sharp):
    n_col, n_bulk = lax.axis_size("col"), lax.axis_size("bulk")
    scale = 1.0 / math.sqrt(x.shape[1] * x.shape[2] * x.shape[3] * n_col * n_bulk)
    place, flags = edge_tables()
    vmem = pl.BlockSpec(memory_space=pltpu.VMEM)
    smem = pl.BlockSpec(memory_space=pltpu.SMEM)
    rows1, rows2 = C // n_bulk, C3 // n_bulk

    def reduction(rows):
        return [
            pltpu.VMEM((n_bulk, rows, LANES), F32),
            pltpu.VMEM((n_bulk, rows, LANES), F32),
            pltpu.VMEM((n_col, rows, LANES), F32),
            pltpu.VMEM((n_bulk, rows, LANES), F32),
        ]

    def dma(count):
        return pltpu.SemaphoreType.DMA((count,))

    reduction_sems = [pltpu.SemaphoreType.DMA] * 6
    dx, pd, kd, sd = pl.pallas_call(
        functools.partial(kernel, (n_col, n_bulk), scale),
        out_shape=(
            jax.ShapeDtypeStruct((C, 4, 2, LANES), BF16),
            jax.ShapeDtypeStruct((C3, C), F32),
            jax.ShapeDtypeStruct((27, C3), F32),
            jax.ShapeDtypeStruct((2,), F32),
        ),
        in_specs=[vmem, vmem, vmem, vmem, smem, vmem, vmem],
        out_specs=(vmem, vmem, vmem, smem),
        scratch_shapes=[
            pltpu.VMEM((2, 4, C, LANES), BF16),
            pltpu.VMEM((2, 4, C, LANES), BF16),
            pltpu.VMEM((4, 4, C, LANES), BF16),
            pltpu.VMEM((2, 4, C, LANES), BF16),
            pltpu.VMEM((2, 32, LANES), BF16),
            pltpu.VMEM((9, 2, 32, LANES), BF16),
            pltpu.VMEM((4, LANES, LANES), BF16),
            pltpu.VMEM((LANES, LANES), F32),
            pltpu.VMEM((LANES, LANES), BF16),
            pltpu.VMEM((LANES, 3 * LANES), F32),
            pltpu.VMEM((3 * LANES, LANES), F32),
            pltpu.VMEM((27, C3, LANES), F32),
            pltpu.VMEM((3, 6, 4, C3, LANES), F32),
            pltpu.VMEM((3, C3, LANES), F32),
            pltpu.VMEM((4, 4, C3, LANES), BF16),
            pltpu.VMEM((C3, LANES), BF16),
            pltpu.VMEM((3, 4, 4, C3, LANES), F32),
            pltpu.VMEM((C3, LANES), F32),
            pltpu.VMEM((2, 4, C3, LANES), BF16),
            pltpu.VMEM((LANES, LANES), F32),
            pltpu.VMEM((3, C, LANES), BF16),
            pltpu.VMEM((2, C, LANES), F32),
            pltpu.VMEM((C, LANES), F32),
            pltpu.VMEM((C3, LANES), F32),
        ]
        + reduction(rows1)
        + reduction(rows2)
        + [dma(6), dma(6), dma(9), dma(9)]
        + reduction_sems
        + reduction_sems,
        compiler_params=pltpu.CompilerParams(
            collective_id=0, has_side_effects=True, vmem_limit_bytes=56 * 2**20
        ),
    )(
        x,
        g,
        w,
        k.T,
        sharp,
        jnp.asarray(place, BF16),
        jnp.asarray(flags),
    )
    dx, pd, kd, sd = pl.pallas_call(
        hand_out,
        out_shape=tuple(jax.ShapeDtypeStruct(v.shape, v.dtype) for v in (dx, pd, kd, sd)),
        in_specs=[vmem, vmem, vmem, smem],
        out_specs=(vmem, vmem, vmem, smem),
    )(dx, pd, kd, sd)
    return dx, pd, kd.T, sd


def solution(mesh):
    return jax.shard_map(
        local,
        mesh=mesh,
        in_specs=(P(None, None, "bulk", "col"), P(None, None, "bulk", "col"), P(), P(), P()),
        out_specs=(P(None, None, "bulk", "col"), P(), P(), P()),
        check_vma=False,
    )
```

```python
import functools
import math

import jax
import jax.numpy as jnp
import numpy as np
from jax import lax
from jax.experimental import pallas as pl
from jax.experimental.pallas import tpu as pltpu
from jax.sharding import PartitionSpec as P

MESH = pl.DeviceIdType.MESH
F32 = jnp.float32
BF16 = jnp.bfloat16
C = 96
HEAD = 48
C3 = 3 * C
LANES = 128
CHUNK = 32
EARLY_TAPS = 10
EDGE_COLUMNS = (0, 1, LANES - 2, LANES - 1)
NEIGHBOURS = [(a, b) for a in (-1, 0, 1) for b in (-1, 0, 1)]


def slot_of(a, b):
    return 3 * (a + 1) + b + 1


def edge_index(z, y):
    return (z + 1) * 6 + y + 2


def edge_tables():
    place = np.zeros((3, LANES, 9 * 32), np.float32)
    flags = np.zeros((8, LANES), np.float32)
    for (a, b) in NEIGHBOURS:
        for s, column in enumerate(EDGE_COLUMNS):
            x = LANES * a + column
            for y in range(2):
                for z in range(4):
                    k = slot_of(a, b) * 32 + s * 8 + y * 4 + z
                    index = 2 * edge_index(z, 2 * b + y)
                    for c in (-1, 0, 1):
                        if x == -1 + c:
                            place[c + 1, index + 1, k] = 1.0
                        if x == LANES + c:
                            place[c + 1, index, k] = 1.0
    for z in range(4):
        for y in range(-1, 3):
            for left in range(2):
                lane = 2 * edge_index(z, y) + left
                flags[0, lane] = 1.0
                flags[1, lane] = left
                flags[2, lane] = 1 - left
                flags[3, lane] = y == -1
                flags[4, lane] = y == 2
    return place.reshape(3 * LANES, 9 * 32), flags


def dot_nt(a, b):
    return lax.dot_general(a, b, (((1,), (1,)), ((), ())), preferred_element_type=F32)


def dot_tn(a, b):
    return lax.dot_general(a, b, (((0,), (0,)), ((), ())), preferred_element_type=F32)


def dot(a, b):
    return jnp.dot(a, b, preferred_element_type=F32)


def iota(shape, dim):
    return lax.broadcasted_iota(jnp.int32, shape, dim)


def rounded(v):
    return v.astype(BF16).astype(F32)


def remote(src, dst, send, recv, target):
    return pltpu.make_async_remote_copy(
        src_ref=src, dst_ref=dst, send_sem=send, recv_sem=recv, device_id=target, device_id_type=MESH
    )


def ring_distance(step, count):
    return min(step, count - step)


def bulk_peers(bulk, n_bulk):
    if n_bulk != 32:
        return [lax.rem(bulk + step, n_bulk) for step in range(1, n_bulk)]
    ys = [lax.rem(bulk // 8 + d, 4) * 8 for d in range(4)]
    xs = [lax.rem(lax.rem(bulk // 2, 4) + d, 4) * 2 for d in range(4)]
    cores = [lax.rem(bulk + d, 2) for d in range(2)]
    steps = [(y, x, c) for y in range(4) for x in range(4) for c in range(2)][1:]
    steps.sort(key=lambda t: -2 * ring_distance(t[0], 4) - 2 * ring_distance(t[1], 4) - t[2])
    return [ys[y] + xs[x] + cores[c] for y, x, c in steps]


def col_peers(col, n_col):
    steps = sorted(range(1, n_col), key=lambda d: -ring_distance(d, n_col))
    return [lax.rem(col + d, n_col) for d in steps]


class Reduction:
    def __init__(self, place, peers, pack, parts, planes, whole, sems):
        self.col, self.bulk = place
        self.in_plane, self.in_col = peers
        self.pack, self.parts, self.planes, self.whole = pack, parts, planes, whole
        self.s_send, self.s_recv, self.z_send, self.z_recv, self.g_send, self.g_recv = sems

    def scattered(self):
        rest = pl.ds(0, len(self.in_plane))
        target = (self.col, self.in_plane[0])
        return remote(self.pack.at[rest], self.parts.at[rest], self.s_send, self.s_recv, target)

    def crossed(self):
        rest = pl.ds(0, len(self.in_col))
        target = (self.in_col[0], self.bulk)
        return remote(self.planes.at[rest], self.planes.at[rest], self.z_send, self.z_recv, target)

    def gathered(self):
        rest = pl.ds(0, len(self.in_plane))
        target = (self.col, self.in_plane[0])
        return remote(self.whole.at[rest], self.whole.at[rest], self.g_send, self.g_recv, target)

    def start(self):
        for peer in self.in_plane:
            remote(
                self.pack.at[peer], self.parts.at[self.bulk], self.s_send, self.s_recv, (self.col, peer)
            ).start()
        self.parts[self.bulk] = self.pack[self.bulk]

    def middle(self):
        self.scattered().wait_recv()
        self.planes[self.col] = jnp.sum(self.parts[...], axis=0)
        mine = self.planes.at[self.col]
        for peer in self.in_col:
            remote(mine, mine, self.z_send, self.z_recv, (peer, self.bulk)).start()

    def final(self):
        self.crossed().wait_recv()
        self.whole[self.bulk] = jnp.sum(self.planes[...], axis=0)
        mine = self.whole.at[self.bulk]
        for peer in self.in_plane:
            remote(mine, mine, self.g_send, self.g_recv, (self.col, peer)).start()

    def finish(self):
        self.gathered().wait_recv()

    def drain(self):
        self.scattered().wait_send()
        self.crossed().wait_send()
        self.gathered().wait_send()


def conv(source, y0, weights, flip, sink, bs=(0, 1, 2), start=None):
    def body(j, carry):
        rows = pl.ds(pl.multiple_of(j * CHUNK, CHUNK), CHUNK)
        total = [None if start is None else start(z, rows) for z in range(4)]
        for b in bs:
            for c in range(3):
                cells = [source[c, y0 + b, z, rows, :] for z in range(4)]
                for a in range(3):
                    tap = 9 * a + 3 * b + c
                    weight = weights[26 - tap if flip else tap, rows, :]
                    for z in range(4):
                        if 0 <= z + a - 1 < 4:
                            term = weight * cells[z + a - 1]
                            total[z] = term if total[z] is None else total[z] + term
        for z in range(4):
            sink(z, rows, total[z])
        return carry

    lax.fori_loop(0, C3 // CHUNK, body, 0)


def kernel(
    sizes,
    scale,
    x_hbm,
    g_hbm,
    w_hbm,
    k_hbm,
    sharp_ref,
    place_hbm,
    flags_ref,
    dx_ref,
    pd_ref,
    kd_ref,
    sd_ref,
    x_in,
    g_in,
    w_ref,
    k_ref,
    place_ref,
    load_sem,
    x_ref,
    g_ref,
    xh,
    gh,
    messages,
    arrived,
    edge_t,
    edge_x,
    edge_g,
    taps_t,
    taps_c,
    weights,
    field,
    field_edge,
    mixed,
    mixed_edge,
    grads,
    grads_edge,
    field_grad,
    turn,
    partial,
    couple,
    coef,
    pay1,
    pay2,
    pack1,
    parts1,
    planes1,
    whole1,
    pack2,
    parts2,
    planes2,
    whole2,
    row_send,
    row_recv,
    edge_send,
    edge_recv,
    *sems,
):
    n_col, n_bulk = sizes
    col, bulk = lax.axis_index("col"), lax.axis_index("bulk")
    peers = bulk_peers(bulk, n_bulk), col_peers(col, n_col)
    first = Reduction((col, bulk), peers, pack1, parts1, planes1, whole1, sems[:6])
    second = Reduction((col, bulk), peers, pack2, parts2, planes2, whole2, sems[6:])
    low, high = bulk > 0, bulk < n_bulk - 1

    loads = [
        pltpu.make_async_copy(source, target, load_sem.at[i])
        for i, (source, target) in enumerate(
            ((x_hbm, x_in), (g_hbm, g_in), (w_hbm, w_ref), (k_hbm, k_ref), (place_hbm, place_ref))
        )
    ]
    for load in loads:
        load.start()

    xh[...] = jnp.zeros_like(xh)
    gh[...] = jnp.zeros_like(gh)
    arrived[...] = jnp.zeros_like(arrived)
    barrier = pltpu.get_barrier_semaphore()

    def greet(target):
        pl.semaphore_signal(barrier, inc=1, device_id=target, device_id_type=MESH)

    for a in (1, n_col - 1):
        for b in (1, n_bulk - 1):
            greet((lax.rem(col + a, n_col), lax.rem(bulk + b, n_bulk)))
    for peer in reversed(peers[1]):
        greet((peer, bulk))
    for peer in reversed(peers[0]):
        greet((col, peer))

    row32, lane32 = iota((32, LANES), 0), iota((32, LANES), 1)

    def take_in(kind):
        source, planes = (x_in, g_in)[kind], (x_ref, g_ref)[kind]
        loads[kind].wait()
        for z in range(4):
            pair = source[:, z].astype(F32)
            for y in range(2):
                planes[y, z] = pair[:, y, :].astype(BF16)

    def make_messages(kind):
        planes = (x_ref, g_ref)[kind]
        total = jnp.zeros((32, C), F32)
        for y in range(2):
            for z in range(4):
                pick = jnp.zeros((32, LANES), jnp.bool_)
                for s, column in enumerate(EDGE_COLUMNS):
                    pick = pick | ((row32 == s * 8 + y * 4 + z) & (lane32 == column))
                total = total + dot_nt(jnp.where(pick, 1.0, 0.0).astype(BF16), planes[y, z])
        messages[kind] = jnp.zeros((32, LANES), BF16)
        messages[kind, :, 0:C] = total.astype(BF16)

    take_in(0)
    make_messages(0)

    loads[3].wait()
    taps_t[...] = jnp.zeros_like(taps_t)
    taps_t[0:27, 0:C3] = k_ref[...]
    for j in range(3):
        taps_c[LANES * j : LANES * (j + 1), :] = taps_t[:, LANES * j : LANES * (j + 1)].T

    def spread_taps(which):
        for t in which:
            weights[t] = jnp.broadcast_to(taps_c[0:C3, t : t + 1], (C3, LANES))

    spread_taps(range(EARLY_TAPS))
    pl.semaphore_wait(barrier, n_bulk + n_col - 2 + 4)

    def row_copy(k, down):
        y = 1 if down == (k != 1) else 0
        if k == 2:
            source, target = g_ref.at[y], gh.at[0 if down else 1]
        else:
            source, target = x_ref.at[y], xh.at[(1, 0)[k] if down else (2, 3)[k]]
        sem = 2 * k + (1 if down else 0)
        return remote(source, target, row_send.at[sem], row_recv.at[sem], (col, lax.rem(bulk + (1 if down else n_bulk - 1), n_bulk)))

    def edge_copy(kind, a, b):
        slot = slot_of(-a, -b)
        target = (lax.rem(col + a + n_col, n_col), lax.rem(bulk + b + n_bulk, n_bulk))
        sem = 9 * kind + slot
        return remote(messages.at[kind], arrived.at[kind, slot], edge_send.at[sem], edge_recv.at[sem], target)

    def inside(a, b):
        return (col + a >= 0) & (col + a < n_col) & (bulk + b >= 0) & (bulk + b < n_bulk)

    around = [(a, b) for (a, b) in NEIGHBOURS if (a, b) != (0, 0)]
    around.sort(key=lambda t: -abs(t[0]) - abs(t[1]))

    def send_edges(kind):
        for (a, b) in around:
            pl.when(inside(a, b))(lambda a=a, b=b: edge_copy(kind, a, b).start())
        arrived[kind, slot_of(0, 0)] = messages[kind]

    def wait_edges(kind):
        for (a, b) in around:
            pl.when(inside(a, b))(lambda a=a, b=b: edge_copy(kind, -a, -b).wait_recv())

    def send_row(k):
        pl.when(high)(lambda: row_copy(k, True).start())
        pl.when(low)(lambda: row_copy(k, False).start())

    send_edges(0)
    send_row(0)

    def wait_row(k):
        pl.when(low)(lambda: row_copy(k, True).wait_recv())
        pl.when(high)(lambda: row_copy(k, False).wait_recv())

    def turned(values, z, y):
        return pltpu.roll(values, LANES - 1 - 2 * edge_index(z, y), 1)

    def shifted(values, edge):
        lane = iota(values.shape, 1)
        before = jnp.where(lane == 0, edge, pltpu.roll(values, 1, 1))
        after = jnp.where(lane == LANES - 1, edge, pltpu.roll(values, LANES - 1, 1))
        return before, after

    def input_row(y):
        return x_ref.at[y] if y in (0, 1) else xh.at[{-2: 0, -1: 1, 2: 2, 3: 3}[y]]

    def make_field(ys, edged):
        for y in ys:
            for z in range(4):
                plane = input_row(y)[z]
                wide = plane.astype(F32)
                edge = turned(edge_x[0:C, :], z, y) if edged else 0.0
                before, after = shifted(wide, edge)
                cells = jnp.concatenate([before.astype(BF16), plane, after.astype(BF16)], axis=1)
                made = rounded(dot(w_ref[...], cells))
                for c in range(3):
                    field[c, y + 2, z] = made[:, LANES * c : LANES * (c + 1)]

    def gather(y, bs, start):
        def sink(z, rows, value):
            partial[y, z, rows, :] = value

        conv(field, y + 1, weights, False, sink, bs, start)

    def make_mixed(y):
        def sink(z, rows, value):
            mixed[y + 1, z, rows, :] = value.astype(BF16)

        conv(field, y + 1, weights, False, sink)

    for load in (loads[2], loads[4]):
        load.wait()
    spread_taps(range(EARLY_TAPS, 27))

    make_field((0, 1), False)
    gather(0, (1, 2), None)
    gather(1, (0, 1), None)
    take_in(1)
    wait_row(0)
    for k in (1, 2):
        send_row(k)
    make_field((-1, 2), False)
    gather(0, (0,), lambda z, rows: partial[0, z, rows, :])
    gather(1, (2,), lambda z, rows: partial[1, z, rows, :])
    wait_edges(0)

    def placed(c, kind):
        return dot(place_ref[LANES * c : LANES * (c + 1), :], arrived[kind].reshape(9 * 32, LANES)).astype(BF16)

    eye = jnp.where(iota((LANES, LANES), 0) == iota((LANES, LANES), 1), 1.0, 0.0).astype(BF16)
    edge_t[1] = placed(1, 0)
    field_edge[1] = rounded(dot_nt(w_ref[...], edge_t[1, :, 0:C]))

    lane = iota((C, LANES), 1)
    left = lax.rem(lane, 2) == 1
    outer = (lane == 0) | (lane == LANES - 1)
    for j in range(3):
        rows = slice(C * j, C * (j + 1))
        beside = field_edge[1, rows, :]
        along_y = [pltpu.roll(beside, 2, 1), beside, pltpu.roll(beside, LANES - 2, 1)]
        along_z = []
        for a in range(3):
            part = None
            for b in range(3):
                tap = 9 * a + 3 * b
                term = jnp.where(left, weights[tap, rows, :], weights[tap + 2, rows, :]) * along_y[b]
                part = term if part is None else part + term
            along_z.append(part)
        part = along_z[1] + (pltpu.roll(along_z[0], 12, 1) + pltpu.roll(along_z[2], LANES - 12, 1))
        for y in range(2):
            for z in range(4):
                value = partial[y, z, rows, :] + jnp.where(outer, turned(part, z, y), 0.0)
                mixed[y + 1, z, rows, :] = value.astype(BF16)

    row, lane = iota((C, LANES), 0), iota((C, LANES), 1)
    upper = row < HEAD
    gram = jnp.zeros((C, LANES), F32)
    value = jnp.zeros((C, LANES), F32)
    square_q = jnp.zeros((C, LANES), F32)
    square_k = jnp.zeros((C, LANES), F32)
    for y in range(2):
        for z in range(4):
            q, k = mixed[y + 1, z, 0:C, :], mixed[y + 1, z, C : 2 * C, :]
            gram = gram + dot_nt(q, mixed[y + 1, z, C : C + LANES, :])
            value = value + dot_nt(g_ref[y, z], mixed[y + 1, z, C3 - LANES : C3, :])
            square_q = square_q + jnp.square(q.astype(F32))
            square_k = square_k + jnp.square(k.astype(F32))
    gram = jnp.where(upper, gram, pltpu.roll(gram, LANES - HEAD, 1))
    value = jnp.where(upper, pltpu.roll(value, 16, 1), pltpu.roll(value, LANES - 32, 1))
    sum_q = jnp.sum(square_q, axis=1, keepdims=True)
    sum_k = jnp.sum(square_k, axis=1, keepdims=True)
    pay1[...] = jnp.where(
        lane < HEAD,
        gram,
        jnp.where(lane < 2 * HEAD, value, jnp.where(lane == C, sum_q, jnp.where(lane == C + 1, sum_k, 0.0))),
    )
    rows1 = C // n_bulk
    for i in range(n_bulk):
        pack1[i] = pay1[rows1 * i : rows1 * (i + 1), :]
    first.start()

    make_messages(1)
    send_edges(1)
    wait_row(1)
    edge_x[...] = dot_nt(eye, edge_t[1])
    make_field((-2, 3), True)
    for y in range(-1, 3):
        for z in range(4):
            edge = turned(field_edge[1], z, y)
            field[0, y + 2, z, :, 0:1] = edge[:, 0:1]
            field[2, y + 2, z, :, LANES - 1 : LANES] = edge[:, LANES - 1 : LANES]
    for c in (0, 2):
        edge_t[c] = placed(c, 0)
        field_edge[c] = rounded(dot_nt(w_ref[...], edge_t[c, :, 0:C]))
    for j in range(3):
        rows = slice(C * j, C * (j + 1))
        along_z = []
        for a in range(3):
            along_y = []
            for b in range(3):
                part = None
                for c in range(3):
                    term = weights[9 * a + 3 * b + c, rows, :] * field_edge[c, rows, :]
                    part = term if part is None else part + term
                along_y.append(part)
            along_z.append(
                along_y[1] + (pltpu.roll(along_y[0], 2, 1) + pltpu.roll(along_y[2], LANES - 2, 1))
            )
        part = along_z[1] + (pltpu.roll(along_z[0], 12, 1) + pltpu.roll(along_z[2], LANES - 12, 1))
        mixed_edge[rows, :] = part.astype(BF16)
    first.middle()
    make_mixed(-1)
    make_mixed(2)
    first.final()
    wait_row(2)
    wait_edges(1)
    edge_t[3] = placed(1, 1)
    edge_g[...] = dot_nt(eye, edge_t[3]).astype(BF16)
    first.finish()

    for i in range(n_bulk):
        pay1[rows1 * i : rows1 * (i + 1), :] = whole1[i]
    sums = pay1[...]
    value = pltpu.roll(sums, LANES - HEAD, 1)
    inv_q = 1.0 / jnp.sqrt(sums[:, C : C + 1] + 1e-06)
    inv_k = 1.0 / jnp.sqrt(sums[:, C + 1 : C + 2] + 1e-06)
    inv_k0 = jnp.sum(jnp.where(row == lane, inv_k, 0.0), axis=0, keepdims=True)
    inv_k1 = jnp.sum(jnp.where(row == lane + HEAD, inv_k, 0.0), axis=0, keepdims=True)
    inv_kr = jnp.where(upper, inv_k0, inv_k1)
    inner = lane < HEAD
    sharp = jnp.where(upper, sharp_ref[0], sharp_ref[1])
    cosine = jnp.where(inner, sums * inv_q * inv_kr, 0.0)
    numerators = jnp.where(inner, jnp.exp(sharp * cosine), 0.0)
    attention = numerators / jnp.sum(numerators, axis=1, keepdims=True)
    score = attention * (value - jnp.sum(attention * value, axis=1, keepdims=True))
    by_cosine = score * cosine
    sd_ref[0] = jnp.sum(jnp.where(upper, by_cosine, 0.0)) * scale
    sd_ref[1] = jnp.sum(jnp.where(upper, 0.0, by_cosine)) * scale
    cosine_grad = sharp * score
    diagonal = cosine_grad * cosine
    diag_q = jnp.sum(diagonal, axis=1, keepdims=True)
    coupling = rounded(inv_q * cosine_grad * inv_kr)

    def blocks(v):
        return jnp.where(
            upper, jnp.where(inner, v, 0.0), jnp.where((lane >= HEAD) & (lane < C), pltpu.roll(v, HEAD, 1), 0.0)
        )

    def transposed(v):
        turn[0:C, :] = v
        turn[C:LANES, :] = jnp.zeros((LANES - C, LANES), F32)
        return turn[...].T

    coupled = blocks(coupling)
    couple[0] = coupled.astype(BF16)
    couple[1] = transposed(coupled)[0:C, :].astype(BF16)
    couple[2] = transposed(blocks(attention))[0:C, :].astype(BF16)
    diag_k = jnp.sum(transposed(blocks(diagonal)), axis=1, keepdims=True)[0:C, :]
    coef[0] = jnp.broadcast_to(inv_q * inv_q * diag_q, (C, LANES))
    coef[1] = jnp.broadcast_to(inv_k * inv_k * diag_k, (C, LANES))

    def gradients(q, k, g):
        grad_q = dot(couple[0, :, 0:C], k) - coef[0] * q.astype(F32)
        grad_k = dot(couple[1, :, 0:C], q) - coef[1] * k.astype(F32)
        return grad_q, grad_k, dot(couple[2, :, 0:C], g)

    def flag(condition):
        return jnp.where(condition, 1.0, 0.0)

    mask = (
        flags_ref[0:1, :]
        * (1.0 - flags_ref[1:2, :] * flag(col == 0))
        * (1.0 - flags_ref[2:3, :] * flag(col == n_col - 1))
        * (1.0 - flags_ref[3:4, :] * flag(bulk == 0))
        * (1.0 - flags_ref[4:5, :] * flag(bulk == n_bulk - 1))
    )
    edges = gradients(mixed_edge[0:C, :], mixed_edge[C : 2 * C, :], edge_g[0:C, :])
    for part in range(3):
        grads_edge[C * part : C * (part + 1), :] = jnp.where(mask > 0.5, rounded(edges[part]), 0.0)

    def grad_planes(z):
        for y in range(-1, 3):
            g = g_ref[y, z] if y in (0, 1) else gh[0 if y == -1 else 1, z]
            made = gradients(mixed[y + 1, z, 0:C, :], mixed[y + 1, z, C : 2 * C, :], g)
            for part in range(3):
                rows = slice(C * part, C * (part + 1))
                plane = rounded(made[part])
                if y == -1:
                    plane = plane * flag(low)
                if y == 2:
                    plane = plane * flag(high)
                before, after = shifted(plane, turned(grads_edge[rows, :], z, y))
                grads[0, y + 1, z, rows, :] = before
                grads[1, y + 1, z, rows, :] = plane
                grads[2, y + 1, z, rows, :] = after

    for z in range(4):
        grad_planes(z)

    for y in range(2):

        def sink(z, rows, value, y=y):
            field_grad[y, z, rows, :] = value.astype(BF16)

        conv(grads, y, weights, True, sink)

    def depth(j, carry):
        rows = pl.ds(pl.multiple_of(j * CHUNK, CHUNK), CHUNK)
        lane = iota((CHUNK, LANES), 1)
        made = jnp.zeros((CHUNK, LANES), F32)
        weight = jnp.zeros((CHUNK, C), F32)
        for y in range(2):
            for z in range(4):
                weight = weight + dot_nt(field_grad[y, z, rows, :], x_ref[y, z])
        for b in range(3):
            for c in range(3):
                for a in range(3):
                    total = None
                    for y in range(2):
                        for z in range(4):
                            if 0 <= z + a - 1 < 4:
                                term = grads[1, y + 1, z, rows, :] * field[c, y + b + 1, z + a - 1, rows, :]
                                total = term if total is None else total + term
                    tap = 9 * a + 3 * b + c
                    made = jnp.where(lane == C + tap, jnp.sum(total, axis=1, keepdims=True), made)
        pay2[rows, :] = made
        pay2[rows, 0:C] = weight
        return carry

    lax.fori_loop(0, C3 // CHUNK, depth, 0)
    rows2 = C3 // n_bulk
    for i in range(n_bulk):
        pack2[i] = pay2[rows2 * i : rows2 * (i + 1), :]
    second.start()

    for z in range(4):
        rows_y = [dot_tn(w_ref[...], field_grad[y, z]) for y in range(2)]
        dx_ref[:, z] = jnp.stack(rows_y, axis=1).astype(BF16)
    for k in range(3):
        pl.when(high)(lambda k=k: row_copy(k, True).wait_send())
        pl.when(low)(lambda k=k: row_copy(k, False).wait_send())
    for kind in range(2):
        for (a, b) in around:
            pl.when(inside(a, b))(lambda a=a, b=b, kind=kind: edge_copy(kind, a, b).wait_send())
    first.drain()
    second.middle()
    second.final()
    second.finish()
    for i in range(n_bulk):
        pay2[rows2 * i : rows2 * (i + 1), :] = whole2[i]
    pd_ref[...] = pay2[:, 0:C] * scale
    taps_c[0:C3, :] = pay2[...] * scale
    for j in range(3):
        taps_t[:, LANES * j : LANES * (j + 1)] = taps_c[LANES * j : LANES * (j + 1), :].T
    kd_ref[...] = taps_t[C : C + 27, 0:C3]
    second.drain()


def hand_out(dx_in, pd_in, kd_in, sd_in, dx_ref, pd_ref, kd_ref, sd_ref):
    dx_ref[...] = dx_in[...]
    pd_ref[...] = pd_in[...]
    kd_ref[...] = kd_in[...]
    for e in range(2):
        sd_ref[e] = sd_in[e]


def local(x, g, w, k, sharp):
    n_col, n_bulk = lax.axis_size("col"), lax.axis_size("bulk")
    scale = 1.0 / math.sqrt(x.shape[1] * x.shape[2] * x.shape[3] * n_col * n_bulk)
    place, flags = edge_tables()
    vmem = pl.BlockSpec(memory_space=pltpu.VMEM)
    smem = pl.BlockSpec(memory_space=pltpu.SMEM)
    hbm = pl.BlockSpec(memory_space=pl.ANY)
    rows1, rows2 = C // n_bulk, C3 // n_bulk

    def reduction(rows):
        return [
            pltpu.VMEM((n_bulk, rows, LANES), F32),
            pltpu.VMEM((n_bulk, rows, LANES), F32),
            pltpu.VMEM((n_col, rows, LANES), F32),
            pltpu.VMEM((n_bulk, rows, LANES), F32),
        ]

    def dma(count):
        return pltpu.SemaphoreType.DMA((count,))

    reduction_sems = [pltpu.SemaphoreType.DMA] * 6
    dx, pd, kd, sd = pl.pallas_call(
        functools.partial(kernel, (n_col, n_bulk), scale),
        out_shape=(
            jax.ShapeDtypeStruct((C, 4, 2, LANES), BF16),
            jax.ShapeDtypeStruct((C3, C), F32),
            jax.ShapeDtypeStruct((27, C3), F32),
            jax.ShapeDtypeStruct((2,), F32),
        ),
        in_specs=[hbm, hbm, hbm, hbm, smem, hbm, vmem],
        out_specs=(vmem, vmem, vmem, smem),
        scratch_shapes=[
            pltpu.VMEM(x.shape, BF16),
            pltpu.VMEM(g.shape, BF16),
            pltpu.VMEM(w.shape, BF16),
            pltpu.VMEM((27, C3), F32),
            pltpu.VMEM(place.shape, BF16),
            pltpu.SemaphoreType.DMA((5,)),
            pltpu.VMEM((2, 4, C, LANES), BF16),
            pltpu.VMEM((2, 4, C, LANES), BF16),
            pltpu.VMEM((4, 4, C, LANES), BF16),
            pltpu.VMEM((2, 4, C, LANES), BF16),
            pltpu.VMEM((2, 32, LANES), BF16),
            pltpu.VMEM((2, 9, 32, LANES), BF16),
            pltpu.VMEM((4, LANES, LANES), BF16),
            pltpu.VMEM((LANES, LANES), F32),
            pltpu.VMEM((LANES, LANES), BF16),
            pltpu.VMEM((LANES, 3 * LANES), F32),
            pltpu.VMEM((3 * LANES, LANES), F32),
            pltpu.VMEM((27, C3, LANES), F32),
            pltpu.VMEM((3, 6, 4, C3, LANES), F32),
            pltpu.VMEM((3, C3, LANES), F32),
            pltpu.VMEM((4, 4, C3, LANES), BF16),
            pltpu.VMEM((C3, LANES), BF16),
            pltpu.VMEM((3, 4, 4, C3, LANES), F32),
            pltpu.VMEM((C3, LANES), F32),
            pltpu.VMEM((2, 4, C3, LANES), BF16),
            pltpu.VMEM((LANES, LANES), F32),
            pltpu.VMEM((2, 4, C3, LANES), F32),
            pltpu.VMEM((3, C, LANES), BF16),
            pltpu.VMEM((2, C, LANES), F32),
            pltpu.VMEM((C, LANES), F32),
            pltpu.VMEM((C3, LANES), F32),
        ]
        + reduction(rows1)
        + reduction(rows2)
        + [dma(6), dma(6), dma(18), dma(18)]
        + reduction_sems
        + reduction_sems,
        compiler_params=pltpu.CompilerParams(
            collective_id=0, has_side_effects=True, vmem_limit_bytes=56 * 2**20
        ),
    )(
        x,
        g,
        w,
        k.T,
        sharp,
        jnp.asarray(place, BF16),
        jnp.asarray(flags),
    )
    dx, pd, kd, sd = pl.pallas_call(
        hand_out,
        out_shape=tuple(jax.ShapeDtypeStruct(v.shape, v.dtype) for v in (dx, pd, kd, sd)),
        in_specs=[vmem, vmem, vmem, smem],
        out_specs=(vmem, vmem, vmem, smem),
    )(dx, pd, kd, sd)
    return dx, pd, kd.T, sd


def solution(mesh):
    return jax.shard_map(
        local,
        mesh=mesh,
        in_specs=(P(None, None, "bulk", "col"), P(None, None, "bulk", "col"), P(), P(), P()),
        out_specs=(P(None, None, "bulk", "col"), P(), P(), P()),
        check_vma=False,
    )
```

```python
import functools
import math

import jax
import jax.numpy as jnp
import numpy as np
from jax import lax
from jax.experimental import pallas as pl
from jax.experimental.pallas import tpu as pltpu
from jax.sharding import PartitionSpec as P

MESH = pl.DeviceIdType.MESH
F32 = jnp.float32
BF16 = jnp.bfloat16
C = 96
HEAD = 48
C3 = 3 * C
LANES = 128
CHUNK = 32
EARLY_TAPS = 10
EDGE_COLUMNS = (0, 1, LANES - 2, LANES - 1)
NEIGHBOURS = [(a, b) for a in (-1, 0, 1) for b in (-1, 0, 1)]


def slot_of(a, b):
    return 3 * (a + 1) + b + 1


def edge_index(z, y):
    return (z + 1) * 6 + y + 2


def edge_tables():
    place = np.zeros((3, LANES, 9 * 32), np.float32)
    flags = np.zeros((8, LANES), np.float32)
    for (a, b) in NEIGHBOURS:
        for s, column in enumerate(EDGE_COLUMNS):
            x = LANES * a + column
            for y in range(2):
                for z in range(4):
                    k = slot_of(a, b) * 32 + s * 8 + y * 4 + z
                    index = 2 * edge_index(z, 2 * b + y)
                    for c in (-1, 0, 1):
                        if x == -1 + c:
                            place[c + 1, index + 1, k] = 1.0
                        if x == LANES + c:
                            place[c + 1, index, k] = 1.0
    for z in range(4):
        for y in range(-1, 3):
            for left in range(2):
                lane = 2 * edge_index(z, y) + left
                flags[0, lane] = 1.0
                flags[1, lane] = left
                flags[2, lane] = 1 - left
                flags[3, lane] = y == -1
                flags[4, lane] = y == 2
    return place.reshape(3 * LANES, 9 * 32), flags


def dot_nt(a, b):
    return lax.dot_general(a, b, (((1,), (1,)), ((), ())), preferred_element_type=F32)


def dot_tn(a, b):
    return lax.dot_general(a, b, (((0,), (0,)), ((), ())), preferred_element_type=F32)


def dot(a, b):
    return jnp.dot(a, b, preferred_element_type=F32)


def iota(shape, dim):
    return lax.broadcasted_iota(jnp.int32, shape, dim)


def rounded(v):
    return v.astype(BF16).astype(F32)


def remote(src, dst, send, recv, target):
    return pltpu.make_async_remote_copy(
        src_ref=src, dst_ref=dst, send_sem=send, recv_sem=recv, device_id=target, device_id_type=MESH
    )


def ring_distance(step, count):
    return min(step, count - step)


def bulk_peers(bulk, n_bulk):
    if n_bulk != 32:
        return [lax.rem(bulk + step, n_bulk) for step in range(1, n_bulk)]
    ys = [lax.rem(bulk // 8 + d, 4) * 8 for d in range(4)]
    xs = [lax.rem(lax.rem(bulk // 2, 4) + d, 4) * 2 for d in range(4)]
    cores = [lax.rem(bulk + d, 2) for d in range(2)]
    steps = [(y, x, c) for y in range(4) for x in range(4) for c in range(2)][1:]
    steps.sort(key=lambda t: -2 * ring_distance(t[0], 4) - 2 * ring_distance(t[1], 4) - t[2])
    return [ys[y] + xs[x] + cores[c] for y, x, c in steps]


def col_peers(col, n_col):
    steps = sorted(range(1, n_col), key=lambda d: -ring_distance(d, n_col))
    return [lax.rem(col + d, n_col) for d in steps]


class Reduction:
    def __init__(self, place, peers, pack, parts, planes, whole, sems):
        self.col, self.bulk = place
        self.in_plane, self.in_col = peers
        self.pack, self.parts, self.planes, self.whole = pack, parts, planes, whole
        self.s_send, self.s_recv, self.z_send, self.z_recv, self.g_send, self.g_recv = sems

    def scattered(self):
        rest = pl.ds(0, len(self.in_plane))
        target = (self.col, self.in_plane[0])
        return remote(self.pack.at[rest], self.parts.at[rest], self.s_send, self.s_recv, target)

    def crossed(self):
        rest = pl.ds(0, len(self.in_col))
        target = (self.in_col[0], self.bulk)
        return remote(self.planes.at[rest], self.planes.at[rest], self.z_send, self.z_recv, target)

    def gathered(self):
        rest = pl.ds(0, len(self.in_plane))
        target = (self.col, self.in_plane[0])
        return remote(self.whole.at[rest], self.whole.at[rest], self.g_send, self.g_recv, target)

    def start(self):
        for peer in self.in_plane:
            remote(
                self.pack.at[peer], self.parts.at[self.bulk], self.s_send, self.s_recv, (self.col, peer)
            ).start()
        self.parts[self.bulk] = self.pack[self.bulk]

    def middle(self):
        self.scattered().wait_recv()
        self.planes[self.col] = jnp.sum(self.parts[...], axis=0)
        mine = self.planes.at[self.col]
        for peer in self.in_col:
            remote(mine, mine, self.z_send, self.z_recv, (peer, self.bulk)).start()

    def final(self):
        self.crossed().wait_recv()
        self.whole[self.bulk] = jnp.sum(self.planes[...], axis=0)
        mine = self.whole.at[self.bulk]
        for peer in self.in_plane:
            remote(mine, mine, self.g_send, self.g_recv, (self.col, peer)).start()

    def finish(self):
        self.gathered().wait_recv()

    def drain(self):
        self.scattered().wait_send()
        self.crossed().wait_send()
        self.gathered().wait_send()


def conv(source, y0, weights, flip, sink, bs=(0, 1, 2), start=None):
    def body(j, carry):
        rows = pl.ds(pl.multiple_of(j * CHUNK, CHUNK), CHUNK)
        total = [None if start is None else start(z, rows) for z in range(4)]
        for b in bs:
            for c in range(3):
                cells = [source[c, y0 + b, z, rows, :] for z in range(4)]
                for a in range(3):
                    tap = 9 * a + 3 * b + c
                    weight = weights[26 - tap if flip else tap, rows, :]
                    for z in range(4):
                        if 0 <= z + a - 1 < 4:
                            term = weight * cells[z + a - 1]
                            total[z] = term if total[z] is None else total[z] + term
        for z in range(4):
            sink(z, rows, total[z])
        return carry

    lax.fori_loop(0, C3 // CHUNK, body, 0)


def kernel(
    sizes,
    scale,
    x_hbm,
    g_hbm,
    w_hbm,
    k_hbm,
    sharp_ref,
    place_hbm,
    flags_ref,
    dx_ref,
    pd_ref,
    kd_ref,
    x_in,
    g_in,
    w_ref,
    k_ref,
    place_ref,
    load_sem,
    x_ref,
    g_ref,
    xh,
    gh,
    messages,
    arrived,
    edge_t,
    edge_x,
    edge_g,
    taps_t,
    taps_c,
    weights,
    field,
    field_edge,
    mixed,
    mixed_edge,
    grads,
    grads_edge,
    field_grad,
    turn,
    partial,
    couple,
    coef,
    pay1,
    pay2,
    pack1,
    parts1,
    planes1,
    whole1,
    pack2,
    parts2,
    planes2,
    whole2,
    row_send,
    row_recv,
    edge_send,
    edge_recv,
    *sems,
):
    n_col, n_bulk = sizes
    col, bulk = lax.axis_index("col"), lax.axis_index("bulk")
    peers = bulk_peers(bulk, n_bulk), col_peers(col, n_col)
    first = Reduction((col, bulk), peers, pack1, parts1, planes1, whole1, sems[:6])
    second = Reduction((col, bulk), peers, pack2, parts2, planes2, whole2, sems[6:])
    low, high = bulk > 0, bulk < n_bulk - 1

    loads = [
        pltpu.make_async_copy(source, target, load_sem.at[i])
        for i, (source, target) in enumerate(
            ((x_hbm, x_in), (g_hbm, g_in), (w_hbm, w_ref), (k_hbm, k_ref), (place_hbm, place_ref))
        )
    ]
    for i in (3, 0, 2, 1, 4):
        loads[i].start()

    xh[...] = jnp.zeros_like(xh)
    gh[...] = jnp.zeros_like(gh)
    arrived[...] = jnp.zeros_like(arrived)
    barrier = pltpu.get_barrier_semaphore()

    def greet(target):
        pl.semaphore_signal(barrier, inc=1, device_id=target, device_id_type=MESH)

    for peer in peers[0][:10]:
        greet((col, peer))
    for peer in peers[1]:
        greet((peer, bulk))
    for a in (1, n_col - 1):
        for b in (1, n_bulk - 1):
            greet((lax.rem(col + a, n_col), lax.rem(bulk + b, n_bulk)))
    for peer in peers[0][10:]:
        greet((col, peer))
    loads[3].wait()
    taps_t[...] = jnp.zeros_like(taps_t)
    taps_t[0:27, 0:C3] = k_ref[...]
    for j in range(3):
        taps_c[LANES * j : LANES * (j + 1), :] = taps_t[:, LANES * j : LANES * (j + 1)].T

    def spread_taps(which):
        for t in which:
            weights[t] = jnp.broadcast_to(taps_c[0:C3, t : t + 1], (C3, LANES))

    spread_taps(range(EARLY_TAPS))
    row32, lane32 = iota((32, LANES), 0), iota((32, LANES), 1)

    def take_in(kind):
        source, planes = (x_in, g_in)[kind], (x_ref, g_ref)[kind]
        loads[kind].wait()
        for z in range(4):
            pair = source[:, z].astype(F32)
            for y in range(2):
                planes[y, z] = pair[:, y, :].astype(BF16)

    def make_messages(kind):
        planes = (x_ref, g_ref)[kind]
        total = jnp.zeros((32, C), F32)
        for y in range(2):
            for z in range(4):
                pick = jnp.zeros((32, LANES), jnp.bool_)
                for s, column in enumerate(EDGE_COLUMNS):
                    pick = pick | ((row32 == s * 8 + y * 4 + z) & (lane32 == column))
                total = total + dot_nt(jnp.where(pick, 1.0, 0.0).astype(BF16), planes[y, z])
        messages[kind] = jnp.zeros((32, LANES), BF16)
        messages[kind, :, 0:C] = total.astype(BF16)

    take_in(0)
    make_messages(0)

    pl.semaphore_wait(barrier, n_bulk + n_col - 2 + 4)

    def row_copy(k, down):
        y = 1 if down == (k != 1) else 0
        if k == 2:
            source, target = g_ref.at[y], gh.at[0 if down else 1]
        else:
            source, target = x_ref.at[y], xh.at[(1, 0)[k] if down else (2, 3)[k]]
        sem = 2 * k + (1 if down else 0)
        return remote(source, target, row_send.at[sem], row_recv.at[sem], (col, lax.rem(bulk + (1 if down else n_bulk - 1), n_bulk)))

    def edge_copy(kind, a, b):
        slot = slot_of(-a, -b)
        target = (lax.rem(col + a + n_col, n_col), lax.rem(bulk + b + n_bulk, n_bulk))
        sem = 9 * kind + slot
        return remote(messages.at[kind], arrived.at[kind, slot], edge_send.at[sem], edge_recv.at[sem], target)

    def inside(a, b):
        return (col + a >= 0) & (col + a < n_col) & (bulk + b >= 0) & (bulk + b < n_bulk)

    around = [(a, b) for (a, b) in NEIGHBOURS if (a, b) != (0, 0)]
    around.sort(key=lambda t: -abs(t[0]) - abs(t[1]))

    def send_edges(kind):
        for (a, b) in around:
            pl.when(inside(a, b))(lambda a=a, b=b: edge_copy(kind, a, b).start())
        arrived[kind, slot_of(0, 0)] = messages[kind]

    def wait_edges(kind):
        for (a, b) in around:
            pl.when(inside(a, b))(lambda a=a, b=b: edge_copy(kind, -a, -b).wait_recv())

    def send_row(k):
        pl.when(high)(lambda: row_copy(k, True).start())
        pl.when(low)(lambda: row_copy(k, False).start())

    send_edges(0)
    send_row(0)

    def wait_row(k):
        pl.when(low)(lambda: row_copy(k, True).wait_recv())
        pl.when(high)(lambda: row_copy(k, False).wait_recv())

    def turned(values, z, y):
        return pltpu.roll(values, LANES - 1 - 2 * edge_index(z, y), 1)

    def shifted(values, edge):
        lane = iota(values.shape, 1)
        before = jnp.where(lane == 0, edge, pltpu.roll(values, 1, 1))
        after = jnp.where(lane == LANES - 1, edge, pltpu.roll(values, LANES - 1, 1))
        return before, after

    def input_row(y):
        return x_ref.at[y] if y in (0, 1) else xh.at[{-2: 0, -1: 1, 2: 2, 3: 3}[y]]

    def make_field(ys, edged):
        for y in ys:
            for z in range(4):
                plane = input_row(y)[z]
                wide = plane.astype(F32)
                edge = turned(edge_x[0:C, :], z, y) if edged else 0.0
                before, after = shifted(wide, edge)
                cells = jnp.concatenate([before.astype(BF16), plane, after.astype(BF16)], axis=1)
                made = rounded(dot(w_ref[...], cells))
                for c in range(3):
                    field[c, y + 2, z] = made[:, LANES * c : LANES * (c + 1)]

    def gather(y, bs, start):
        def sink(z, rows, value):
            partial[y, z, rows, :] = value

        conv(field, y + 1, weights, False, sink, bs, start)

    def make_mixed(y):
        def sink(z, rows, value):
            mixed[y + 1, z, rows, :] = value.astype(BF16)

        conv(field, y + 1, weights, False, sink)

    for load in (loads[2], loads[4]):
        load.wait()
    spread_taps(range(EARLY_TAPS, 27))

    make_field((0, 1), False)
    gather(0, (1, 2), None)
    gather(1, (0, 1), None)
    take_in(1)
    wait_row(0)
    for k in (1, 2):
        send_row(k)
    make_field((-1, 2), False)
    gather(0, (0,), lambda z, rows: partial[0, z, rows, :])
    gather(1, (2,), lambda z, rows: partial[1, z, rows, :])
    wait_edges(0)

    def placed(c, kind):
        return dot(place_ref[LANES * c : LANES * (c + 1), :], arrived[kind].reshape(9 * 32, LANES)).astype(BF16)

    eye = jnp.where(iota((LANES, LANES), 0) == iota((LANES, LANES), 1), 1.0, 0.0).astype(BF16)
    edge_t[1] = placed(1, 0)
    field_edge[1] = rounded(dot_nt(w_ref[...], edge_t[1, :, 0:C]))

    lane = iota((C, LANES), 1)
    left = lax.rem(lane, 2) == 1
    outer = (lane == 0) | (lane == LANES - 1)
    for j in range(3):
        rows = slice(C * j, C * (j + 1))
        beside = field_edge[1, rows, :]
        along_y = [pltpu.roll(beside, 2, 1), beside, pltpu.roll(beside, LANES - 2, 1)]
        along_z = []
        for a in range(3):
            part = None
            for b in range(3):
                tap = 9 * a + 3 * b
                term = jnp.where(left, weights[tap, rows, :], weights[tap + 2, rows, :]) * along_y[b]
                part = term if part is None else part + term
            along_z.append(part)
        part = along_z[1] + (pltpu.roll(along_z[0], 12, 1) + pltpu.roll(along_z[2], LANES - 12, 1))
        for y in range(2):
            for z in range(4):
                value = partial[y, z, rows, :] + jnp.where(outer, turned(part, z, y), 0.0)
                mixed[y + 1, z, rows, :] = value.astype(BF16)

    row, lane = iota((C, LANES), 0), iota((C, LANES), 1)
    upper = row < HEAD
    gram = jnp.zeros((C, LANES), F32)
    value = jnp.zeros((C, LANES), F32)
    square_q = jnp.zeros((C, LANES), F32)
    square_k = jnp.zeros((C, LANES), F32)
    for y in range(2):
        for z in range(4):
            q, k = mixed[y + 1, z, 0:C, :], mixed[y + 1, z, C : 2 * C, :]
            gram = gram + dot_nt(q, mixed[y + 1, z, C : C + LANES, :])
            value = value + dot_nt(g_ref[y, z], mixed[y + 1, z, C3 - LANES : C3, :])
            square_q = square_q + jnp.square(q.astype(F32))
            square_k = square_k + jnp.square(k.astype(F32))
    gram = jnp.where(upper, gram, pltpu.roll(gram, LANES - HEAD, 1))
    value = jnp.where(upper, pltpu.roll(value, 16, 1), pltpu.roll(value, LANES - 32, 1))
    sum_q = jnp.sum(square_q, axis=1, keepdims=True)
    sum_k = jnp.sum(square_k, axis=1, keepdims=True)
    pay1[...] = jnp.where(
        lane < HEAD,
        gram,
        jnp.where(lane < 2 * HEAD, value, jnp.where(lane == C, sum_q, jnp.where(lane == C + 1, sum_k, 0.0))),
    )
    rows1 = C // n_bulk
    for i in range(n_bulk):
        pack1[i] = pay1[rows1 * i : rows1 * (i + 1), :]
    first.start()

    make_messages(1)
    send_edges(1)
    wait_row(1)
    edge_x[...] = dot_nt(eye, edge_t[1])
    make_field((-2, 3), True)
    for y in range(-1, 3):
        for z in range(4):
            edge = turned(field_edge[1], z, y)
            field[0, y + 2, z, :, 0:1] = edge[:, 0:1]
            field[2, y + 2, z, :, LANES - 1 : LANES] = edge[:, LANES - 1 : LANES]
    for c in (0, 2):
        edge_t[c] = placed(c, 0)
        field_edge[c] = rounded(dot_nt(w_ref[...], edge_t[c, :, 0:C]))
    for j in range(3):
        rows = slice(C * j, C * (j + 1))
        along_z = []
        for a in range(3):
            along_y = []
            for b in range(3):
                part = None
                for c in range(3):
                    term = weights[9 * a + 3 * b + c, rows, :] * field_edge[c, rows, :]
                    part = term if part is None else part + term
                along_y.append(part)
            along_z.append(
                along_y[1] + (pltpu.roll(along_y[0], 2, 1) + pltpu.roll(along_y[2], LANES - 2, 1))
            )
        part = along_z[1] + (pltpu.roll(along_z[0], 12, 1) + pltpu.roll(along_z[2], LANES - 12, 1))
        mixed_edge[rows, :] = part.astype(BF16)
    first.middle()
    make_mixed(-1)
    make_mixed(2)
    first.final()
    wait_row(2)
    wait_edges(1)
    edge_t[3] = placed(1, 1)
    edge_g[...] = dot_nt(eye, edge_t[3]).astype(BF16)
    first.finish()

    for i in range(n_bulk):
        pay1[rows1 * i : rows1 * (i + 1), :] = whole1[i]
    sums = pay1[...]
    value = pltpu.roll(sums, LANES - HEAD, 1)
    inv_q = 1.0 / jnp.sqrt(sums[:, C : C + 1] + 1e-06)
    inv_k = 1.0 / jnp.sqrt(sums[:, C + 1 : C + 2] + 1e-06)
    inv_k0 = jnp.sum(jnp.where(row == lane, inv_k, 0.0), axis=0, keepdims=True)
    inv_k1 = jnp.sum(jnp.where(row == lane + HEAD, inv_k, 0.0), axis=0, keepdims=True)
    inv_kr = jnp.where(upper, inv_k0, inv_k1)
    inner = lane < HEAD
    sharp = jnp.where(upper, sharp_ref[0], sharp_ref[1])
    cosine = jnp.where(inner, sums * inv_q * inv_kr, 0.0)
    numerators = jnp.where(inner, jnp.exp(sharp * cosine), 0.0)
    attention = numerators / jnp.sum(numerators, axis=1, keepdims=True)
    score = attention * (value - jnp.sum(attention * value, axis=1, keepdims=True))
    by_cosine = score * cosine
    for e in range(2):
        total = jnp.sum(jnp.where(upper if e == 0 else ~upper, by_cosine, 0.0), axis=1, keepdims=True)
        kd_ref[27 + e : 28 + e, :] = jnp.broadcast_to(jnp.sum(total, axis=0, keepdims=True) * scale, (1, C3))
    cosine_grad = sharp * score
    diagonal = cosine_grad * cosine
    diag_q = jnp.sum(diagonal, axis=1, keepdims=True)
    coupling = rounded(inv_q * cosine_grad * inv_kr)

    def blocks(v):
        return jnp.where(
            upper, jnp.where(inner, v, 0.0), jnp.where((lane >= HEAD) & (lane < C), pltpu.roll(v, HEAD, 1), 0.0)
        )

    def transposed(v):
        turn[0:C, :] = v
        turn[C:LANES, :] = jnp.zeros((LANES - C, LANES), F32)
        return turn[...].T

    coupled = blocks(coupling)
    couple[0] = coupled.astype(BF16)
    couple[1] = transposed(coupled)[0:C, :].astype(BF16)
    couple[2] = transposed(blocks(attention))[0:C, :].astype(BF16)
    diag_k = jnp.sum(transposed(blocks(diagonal)), axis=1, keepdims=True)[0:C, :]
    coef[0] = jnp.broadcast_to(inv_q * inv_q * diag_q, (C, LANES))
    coef[1] = jnp.broadcast_to(inv_k * inv_k * diag_k, (C, LANES))

    def gradients(q, k, g):
        grad_q = dot(couple[0, :, 0:C], k) - coef[0] * q.astype(F32)
        grad_k = dot(couple[1, :, 0:C], q) - coef[1] * k.astype(F32)
        return grad_q, grad_k, dot(couple[2, :, 0:C], g)

    def flag(condition):
        return jnp.where(condition, 1.0, 0.0)

    mask = (
        flags_ref[0:1, :]
        * (1.0 - flags_ref[1:2, :] * flag(col == 0))
        * (1.0 - flags_ref[2:3, :] * flag(col == n_col - 1))
        * (1.0 - flags_ref[3:4, :] * flag(bulk == 0))
        * (1.0 - flags_ref[4:5, :] * flag(bulk == n_bulk - 1))
    )
    edges = gradients(mixed_edge[0:C, :], mixed_edge[C : 2 * C, :], edge_g[0:C, :])
    for part in range(3):
        grads_edge[C * part : C * (part + 1), :] = jnp.where(mask > 0.5, rounded(edges[part]), 0.0)

    def grad_planes(z):
        for y in range(-1, 3):
            g = g_ref[y, z] if y in (0, 1) else gh[0 if y == -1 else 1, z]
            made = gradients(mixed[y + 1, z, 0:C, :], mixed[y + 1, z, C : 2 * C, :], g)
            for part in range(3):
                rows = slice(C * part, C * (part + 1))
                plane = rounded(made[part])
                if y == -1:
                    plane = plane * flag(low)
                if y == 2:
                    plane = plane * flag(high)
                before, after = shifted(plane, turned(grads_edge[rows, :], z, y))
                grads[0, y + 1, z, rows, :] = before
                grads[1, y + 1, z, rows, :] = plane
                grads[2, y + 1, z, rows, :] = after

    for z in range(4):
        grad_planes(z)

    for y in range(2):

        def sink(z, rows, value, y=y):
            field_grad[y, z, rows, :] = value.astype(BF16)

        conv(grads, y, weights, True, sink)

    def depth(j, carry):
        rows = pl.ds(pl.multiple_of(j * CHUNK, CHUNK), CHUNK)
        lane = iota((CHUNK, LANES), 1)
        made = jnp.zeros((CHUNK, LANES), F32)
        weight = jnp.zeros((CHUNK, C), F32)
        for y in range(2):
            for z in range(4):
                weight = weight + dot_nt(field_grad[y, z, rows, :], x_ref[y, z])
        for b in range(3):
            for c in range(3):
                for a in range(3):
                    total = None
                    for y in range(2):
                        for z in range(4):
                            if 0 <= z + a - 1 < 4:
                                term = grads[1, y + 1, z, rows, :] * field[c, y + b + 1, z + a - 1, rows, :]
                                total = term if total is None else total + term
                    tap = 9 * a + 3 * b + c
                    made = jnp.where(lane == C + tap, jnp.sum(total, axis=1, keepdims=True), made)
        pay2[rows, :] = made
        pay2[rows, 0:C] = weight
        return carry

    lax.fori_loop(0, C3 // CHUNK, depth, 0)
    rows2 = C3 // n_bulk
    for i in range(n_bulk):
        pack2[i] = pay2[rows2 * i : rows2 * (i + 1), :]
    second.start()

    for z in range(4):
        rows_y = [dot_tn(w_ref[...], field_grad[y, z]) for y in range(2)]
        dx_ref[:, z] = jnp.stack(rows_y, axis=1).astype(BF16)
    for k in range(3):
        pl.when(high)(lambda k=k: row_copy(k, True).wait_send())
        pl.when(low)(lambda k=k: row_copy(k, False).wait_send())
    for kind in range(2):
        for (a, b) in around:
            pl.when(inside(a, b))(lambda a=a, b=b, kind=kind: edge_copy(kind, a, b).wait_send())
    first.drain()
    second.middle()
    second.final()
    second.finish()
    for i in range(n_bulk):
        pay2[rows2 * i : rows2 * (i + 1), :] = whole2[i]
    pd_ref[...] = pay2[:, 0:C] * scale
    taps_c[0:C3, :] = pay2[...] * scale
    for j in range(3):
        taps_t[:, LANES * j : LANES * (j + 1)] = taps_c[LANES * j : LANES * (j + 1), :].T
    kd_ref[0:27, :] = taps_t[C : C + 27, 0:C3]
    second.drain()


def hand_out(dx_in, pd_in, kd_in, dx_ref, pd_ref, kd_ref, sd_ref):
    dx_ref[...] = dx_in[...]
    pd_ref[...] = pd_in[...]
    kd_ref[...] = kd_in[0:27, :]
    for e in range(2):
        sd_ref[e] = kd_in[27 + e, 0]


def local(x, g, w, k, sharp):
    n_col, n_bulk = lax.axis_size("col"), lax.axis_size("bulk")
    scale = 1.0 / math.sqrt(x.shape[1] * x.shape[2] * x.shape[3] * n_col * n_bulk)
    place, flags = edge_tables()
    vmem = pl.BlockSpec(memory_space=pltpu.VMEM)
    smem = pl.BlockSpec(memory_space=pltpu.SMEM)
    hbm = pl.BlockSpec(memory_space=pl.ANY)
    rows1, rows2 = C // n_bulk, C3 // n_bulk

    def reduction(rows):
        return [
            pltpu.VMEM((n_bulk, rows, LANES), F32),
            pltpu.VMEM((n_bulk, rows, LANES), F32),
            pltpu.VMEM((n_col, rows, LANES), F32),
            pltpu.VMEM((n_bulk, rows, LANES), F32),
        ]

    def dma(count):
        return pltpu.SemaphoreType.DMA((count,))

    reduction_sems = [pltpu.SemaphoreType.DMA] * 6
    dx, pd, kd = pl.pallas_call(
        functools.partial(kernel, (n_col, n_bulk), scale),
        out_shape=(
            pltpu.VMEM((C, 4, 2, LANES), BF16),
            pltpu.VMEM((C3, C), F32),
            pltpu.VMEM((32, C3), F32),
        ),
        in_specs=[hbm, hbm, hbm, hbm, smem, hbm, vmem],
        out_specs=(vmem, vmem, vmem),
        scratch_shapes=[
            pltpu.VMEM(x.shape, BF16),
            pltpu.VMEM(g.shape, BF16),
            pltpu.VMEM(w.shape, BF16),
            pltpu.VMEM((27, C3), F32),
            pltpu.VMEM(place.shape, BF16),
            pltpu.SemaphoreType.DMA((5,)),
            pltpu.VMEM((2, 4, C, LANES), BF16),
            pltpu.VMEM((2, 4, C, LANES), BF16),
            pltpu.VMEM((4, 4, C, LANES), BF16),
            pltpu.VMEM((2, 4, C, LANES), BF16),
            pltpu.VMEM((2, 32, LANES), BF16),
            pltpu.VMEM((2, 9, 32, LANES), BF16),
            pltpu.VMEM((4, LANES, LANES), BF16),
            pltpu.VMEM((LANES, LANES), F32),
            pltpu.VMEM((LANES, LANES), BF16),
            pltpu.VMEM((LANES, 3 * LANES), F32),
            pltpu.VMEM((3 * LANES, LANES), F32),
            pltpu.VMEM((27, C3, LANES), F32),
            pltpu.VMEM((3, 6, 4, C3, LANES), F32),
            pltpu.VMEM((3, C3, LANES), F32),
            pltpu.VMEM((4, 4, C3, LANES), BF16),
            pltpu.VMEM((C3, LANES), BF16),
            pltpu.VMEM((3, 4, 4, C3, LANES), F32),
            pltpu.VMEM((C3, LANES), F32),
            pltpu.VMEM((2, 4, C3, LANES), BF16),
            pltpu.VMEM((LANES, LANES), F32),
            pltpu.VMEM((2, 4, C3, LANES), F32),
            pltpu.VMEM((3, C, LANES), BF16),
            pltpu.VMEM((2, C, LANES), F32),
            pltpu.VMEM((C, LANES), F32),
            pltpu.VMEM((C3, LANES), F32),
        ]
        + reduction(rows1)
        + reduction(rows2)
        + [dma(6), dma(6), dma(18), dma(18)]
        + reduction_sems
        + reduction_sems,
        compiler_params=pltpu.CompilerParams(
            collective_id=0, has_side_effects=True, vmem_limit_bytes=56 * 2**20
        ),
    )(
        x,
        g,
        w,
        k.T,
        sharp,
        jnp.asarray(place, BF16),
        jnp.asarray(flags),
    )
    dx, pd, kd, sd = pl.pallas_call(
        hand_out,
        out_shape=(
            jax.ShapeDtypeStruct((C, 4, 2, LANES), BF16),
            jax.ShapeDtypeStruct((C3, C), F32),
            jax.ShapeDtypeStruct((27, C3), F32),
            jax.ShapeDtypeStruct((2,), F32),
        ),
        in_specs=[vmem, vmem, vmem],
        out_specs=(vmem, vmem, vmem, smem),
        compiler_params=pltpu.CompilerParams(vmem_limit_bytes=4 * 2**20),
    )(dx, pd, kd)
    return dx, pd, kd.T, sd


def solution(mesh):
    return jax.shard_map(
        local,
        mesh=mesh,
        in_specs=(P(None, None, "bulk", "col"), P(None, None, "bulk", "col"), P(), P(), P()),
        out_specs=(P(None, None, "bulk", "col"), P(), P(), P()),
        check_vma=False,
    )
```

```python
import functools
import math

import jax
import jax.numpy as jnp
import numpy as np
from jax import lax
from jax.experimental import pallas as pl
from jax.experimental.pallas import tpu as pltpu
from jax.sharding import PartitionSpec as P

MESH = pl.DeviceIdType.MESH
F32 = jnp.float32
BF16 = jnp.bfloat16
C = 96
HEAD = 48
C3 = 3 * C
LANES = 128
CHUNK = 32
DEPTH_CHUNK = 96
EARLY_TAPS = 10
EDGE_COLUMNS = (0, 1, LANES - 2, LANES - 1)
NEIGHBOURS = [(a, b) for a in (-1, 0, 1) for b in (-1, 0, 1)]


def slot_of(a, b):
    return 3 * (a + 1) + b + 1


def edge_index(z, y):
    return (z + 1) * 6 + y + 2


def edge_tables():
    place = np.zeros((3, LANES, 9 * 32), np.float32)
    flags = np.zeros((8, LANES), np.float32)
    for (a, b) in NEIGHBOURS:
        for s, column in enumerate(EDGE_COLUMNS):
            x = LANES * a + column
            for y in range(2):
                for z in range(4):
                    k = slot_of(a, b) * 32 + s * 8 + y * 4 + z
                    index = 2 * edge_index(z, 2 * b + y)
                    for c in (-1, 0, 1):
                        if x == -1 + c:
                            place[c + 1, index + 1, k] = 1.0
                        if x == LANES + c:
                            place[c + 1, index, k] = 1.0
    for z in range(4):
        for y in range(-1, 3):
            for left in range(2):
                lane = 2 * edge_index(z, y) + left
                flags[0, lane] = 1.0
                flags[1, lane] = left
                flags[2, lane] = 1 - left
                flags[3, lane] = y == -1
                flags[4, lane] = y == 2
    return place.reshape(3 * LANES, 9 * 32), flags


def dot_nt(a, b):
    return lax.dot_general(a, b, (((1,), (1,)), ((), ())), preferred_element_type=F32)


def dot_tn(a, b):
    return lax.dot_general(a, b, (((0,), (0,)), ((), ())), preferred_element_type=F32)


def dot(a, b):
    return jnp.dot(a, b, preferred_element_type=F32)


def iota(shape, dim):
    return lax.broadcasted_iota(jnp.int32, shape, dim)


def rounded(v):
    return v.astype(BF16).astype(F32)


def remote(src, dst, send, recv, target):
    return pltpu.make_async_remote_copy(
        src_ref=src, dst_ref=dst, send_sem=send, recv_sem=recv, device_id=target, device_id_type=MESH
    )


def ring_distance(step, count):
    return min(step, count - step)


def bulk_peers(bulk, n_bulk):
    if n_bulk != 32:
        return [lax.rem(bulk + step, n_bulk) for step in range(1, n_bulk)]
    ys = [lax.rem(bulk // 8 + d, 4) * 8 for d in range(4)]
    xs = [lax.rem(lax.rem(bulk // 2, 4) + d, 4) * 2 for d in range(4)]
    cores = [lax.rem(bulk + d, 2) for d in range(2)]
    steps = [(y, x, c) for y in range(4) for x in range(4) for c in range(2)][1:]
    steps.sort(key=lambda t: -2 * ring_distance(t[0], 4) - 2 * ring_distance(t[1], 4) - t[2])
    return [ys[y] + xs[x] + cores[c] for y, x, c in steps]


def col_peers(col, n_col):
    steps = sorted(range(1, n_col), key=lambda d: -ring_distance(d, n_col))
    return [lax.rem(col + d, n_col) for d in steps]


class Reduction:
    def __init__(self, place, peers, pack, parts, planes, whole, sems):
        self.col, self.bulk = place
        self.in_plane, self.in_col = peers
        self.pack, self.parts, self.planes, self.whole = pack, parts, planes, whole
        self.s_send, self.s_recv, self.z_send, self.z_recv, self.g_send, self.g_recv = sems

    def scattered(self):
        rest = pl.ds(0, len(self.in_plane))
        target = (self.col, self.in_plane[0])
        return remote(self.pack.at[rest], self.parts.at[rest], self.s_send, self.s_recv, target)

    def crossed(self):
        rest = pl.ds(0, len(self.in_col))
        target = (self.in_col[0], self.bulk)
        return remote(self.planes.at[rest], self.planes.at[rest], self.z_send, self.z_recv, target)

    def gathered(self):
        rest = pl.ds(0, len(self.in_plane))
        target = (self.col, self.in_plane[0])
        return remote(self.whole.at[rest], self.whole.at[rest], self.g_send, self.g_recv, target)

    def start(self):
        for peer in self.in_plane:
            remote(
                self.pack.at[peer], self.parts.at[self.bulk], self.s_send, self.s_recv, (self.col, peer)
            ).start()
        self.parts[self.bulk] = self.pack[self.bulk]

    def middle(self):
        self.scattered().wait_recv()
        self.planes[self.col] = jnp.sum(self.parts[...], axis=0)
        mine = self.planes.at[self.col]
        for peer in self.in_col:
            remote(mine, mine, self.z_send, self.z_recv, (peer, self.bulk)).start()

    def final(self):
        self.crossed().wait_recv()
        self.whole[self.bulk] = jnp.sum(self.planes[...], axis=0)
        mine = self.whole.at[self.bulk]
        for peer in self.in_plane:
            remote(mine, mine, self.g_send, self.g_recv, (self.col, peer)).start()

    def finish(self):
        self.gathered().wait_recv()

    def drain(self):
        self.scattered().wait_send()
        self.crossed().wait_send()
        self.gathered().wait_send()


def conv(source, y0, weights, flip, sink, bs=(0, 1, 2), start=None):
    def chunk(rows):
        total = [None if start is None else start(z, rows) for z in range(4)]
        for b in bs:
            for c in range(3):
                cells = [source[c, y0 + b, z, rows, :] for z in range(4)]
                for a in range(3):
                    tap = 9 * a + 3 * b + c
                    weight = weights[26 - tap if flip else tap, rows, :]
                    for z in range(4):
                        if 0 <= z + a - 1 < 4:
                            term = weight * cells[z + a - 1]
                            total[z] = term if total[z] is None else total[z] + term
        for z in range(4):
            sink(z, rows, total[z])

    def body(j, carry):
        for h in range(3):
            chunk(pl.ds(pl.multiple_of(j * 3 * CHUNK + h * CHUNK, CHUNK), CHUNK))
        return carry

    lax.fori_loop(0, C3 // (3 * CHUNK), body, 0)


def kernel(
    sizes,
    scale,
    x_hbm,
    g_hbm,
    w_hbm,
    k_hbm,
    sharp_ref,
    place_hbm,
    flags_ref,
    dx_ref,
    pd_ref,
    kd_ref,
    x_in,
    g_in,
    w_ref,
    k_ref,
    place_ref,
    load_sem,
    x_ref,
    g_ref,
    xh,
    gh,
    messages,
    arrived,
    edge_t,
    edge_x,
    edge_g,
    taps_t,
    taps_c,
    weights,
    field,
    field_edge,
    mixed,
    mixed_edge,
    grads,
    grads_edge,
    field_grad,
    turn,
    partial,
    couple,
    coef,
    pay1,
    pay2,
    pack1,
    parts1,
    planes1,
    whole1,
    pack2,
    parts2,
    planes2,
    whole2,
    row_send,
    row_recv,
    edge_send,
    edge_recv,
    *sems,
):
    n_col, n_bulk = sizes
    col, bulk = lax.axis_index("col"), lax.axis_index("bulk")
    peers = bulk_peers(bulk, n_bulk), col_peers(col, n_col)
    first = Reduction((col, bulk), peers, pack1, parts1, planes1, whole1, sems[:6])
    second = Reduction((col, bulk), peers, pack2, parts2, planes2, whole2, sems[6:])
    low, high = bulk > 0, bulk < n_bulk - 1

    loads = [
        pltpu.make_async_copy(source, target, load_sem.at[i])
        for i, (source, target) in enumerate(
            ((x_hbm, x_in), (g_hbm, g_in), (w_hbm, w_ref), (k_hbm, k_ref), (place_hbm, place_ref))
        )
    ]
    for i in (3, 0, 2, 1, 4):
        loads[i].start()

    xh[...] = jnp.zeros_like(xh)
    gh[...] = jnp.zeros_like(gh)
    arrived[...] = jnp.zeros_like(arrived)
    barrier = pltpu.get_barrier_semaphore()

    def greet(target):
        pl.semaphore_signal(barrier, inc=1, device_id=target, device_id_type=MESH)

    for peer in peers[0][:10]:
        greet((col, peer))
    for peer in peers[1]:
        greet((peer, bulk))
    for a in (1, n_col - 1):
        for b in (1, n_bulk - 1):
            greet((lax.rem(col + a, n_col), lax.rem(bulk + b, n_bulk)))
    for peer in peers[0][10:]:
        greet((col, peer))
    loads[3].wait()
    taps_t[...] = jnp.zeros_like(taps_t)
    taps_t[0:27, 0:C3] = k_ref[...]
    for j in range(3):
        taps_c[LANES * j : LANES * (j + 1), :] = taps_t[:, LANES * j : LANES * (j + 1)].T

    def spread_taps(which):
        for t in which:
            weights[t] = jnp.broadcast_to(taps_c[0:C3, t : t + 1], (C3, LANES))

    spread_taps(range(EARLY_TAPS))
    row32, lane32 = iota((32, LANES), 0), iota((32, LANES), 1)

    def take_in(kind):
        source, planes = (x_in, g_in)[kind], (x_ref, g_ref)[kind]
        loads[kind].wait()
        for z in range(4):
            pair = source[:, z].astype(F32)
            for y in range(2):
                planes[y, z] = pair[:, y, :].astype(BF16)

    def make_messages(kind):
        planes = (x_ref, g_ref)[kind]
        total = jnp.zeros((32, C), F32)
        for y in range(2):
            for z in range(4):
                pick = jnp.zeros((32, LANES), jnp.bool_)
                for s, column in enumerate(EDGE_COLUMNS):
                    pick = pick | ((row32 == s * 8 + y * 4 + z) & (lane32 == column))
                total = total + dot_nt(jnp.where(pick, 1.0, 0.0).astype(BF16), planes[y, z])
        messages[kind] = jnp.zeros((32, LANES), BF16)
        messages[kind, :, 0:C] = total.astype(BF16)

    take_in(0)
    make_messages(0)

    pl.semaphore_wait(barrier, n_bulk + n_col - 2 + 4)

    def row_copy(k, down):
        y = 1 if down == (k != 1) else 0
        if k == 2:
            source, target = g_ref.at[y], gh.at[0 if down else 1]
        else:
            source, target = x_ref.at[y], xh.at[(1, 0)[k] if down else (2, 3)[k]]
        sem = 2 * k + (1 if down else 0)
        return remote(source, target, row_send.at[sem], row_recv.at[sem], (col, lax.rem(bulk + (1 if down else n_bulk - 1), n_bulk)))

    def edge_copy(kind, a, b):
        slot = slot_of(-a, -b)
        target = (lax.rem(col + a + n_col, n_col), lax.rem(bulk + b + n_bulk, n_bulk))
        sem = 9 * kind + slot
        return remote(messages.at[kind], arrived.at[kind, slot], edge_send.at[sem], edge_recv.at[sem], target)

    def inside(a, b):
        return (col + a >= 0) & (col + a < n_col) & (bulk + b >= 0) & (bulk + b < n_bulk)

    around = [(a, b) for (a, b) in NEIGHBOURS if (a, b) != (0, 0)]
    around.sort(key=lambda t: -abs(t[0]) - abs(t[1]))

    def send_edges(kind):
        for (a, b) in around:
            pl.when(inside(a, b))(lambda a=a, b=b: edge_copy(kind, a, b).start())
        arrived[kind, slot_of(0, 0)] = messages[kind]

    def wait_edges(kind):
        for (a, b) in around:
            pl.when(inside(a, b))(lambda a=a, b=b: edge_copy(kind, -a, -b).wait_recv())

    def send_row(k):
        pl.when(high)(lambda: row_copy(k, True).start())
        pl.when(low)(lambda: row_copy(k, False).start())

    send_edges(0)
    send_row(0)

    def wait_row(k):
        pl.when(low)(lambda: row_copy(k, True).wait_recv())
        pl.when(high)(lambda: row_copy(k, False).wait_recv())

    def turned(values, z, y):
        return pltpu.roll(values, LANES - 1 - 2 * edge_index(z, y), 1)

    def shifted(values, edge):
        lane = iota(values.shape, 1)
        before = jnp.where(lane == 0, edge, pltpu.roll(values, 1, 1).astype(F32))
        after = jnp.where(lane == LANES - 1, edge, pltpu.roll(values, LANES - 1, 1).astype(F32))
        return before, after

    def input_row(y):
        return x_ref.at[y] if y in (0, 1) else xh.at[{-2: 0, -1: 1, 2: 2, 3: 3}[y]]

    def make_field(ys, edged):
        for y in ys:
            for z in range(4):
                plane = input_row(y)[z]
                edge = turned(edge_x[0:C, :], z, y).astype(F32) if edged else 0.0
                before, after = shifted(plane, edge)
                cells = jnp.concatenate([before.astype(BF16), plane, after.astype(BF16)], axis=1)
                made = rounded(dot(w_ref[...], cells))
                for c in range(3):
                    field[c, y + 2, z] = made[:, LANES * c : LANES * (c + 1)]

    def gather(y, bs, start):
        def sink(z, rows, value):
            partial[y, z, rows, :] = value

        conv(field, y + 1, weights, False, sink, bs, start)

    def make_mixed(y):
        def sink(z, rows, value):
            mixed[y + 1, z, rows, :] = value.astype(BF16)

        conv(field, y + 1, weights, False, sink)

    for load in (loads[2], loads[4]):
        load.wait()
    spread_taps(range(EARLY_TAPS, 27))

    make_field((0, 1), False)
    gather(0, (1, 2), None)
    gather(1, (0, 1), None)
    take_in(1)
    wait_row(0)
    for k in (1, 2):
        send_row(k)
    make_field((-1, 2), False)
    gather(0, (0,), lambda z, rows: partial[0, z, rows, :])
    gather(1, (2,), lambda z, rows: partial[1, z, rows, :])
    wait_edges(0)

    def placed(c, kind):
        return dot(place_ref[LANES * c : LANES * (c + 1), :], arrived[kind].reshape(9 * 32, LANES)).astype(BF16)

    eye = jnp.where(iota((LANES, LANES), 0) == iota((LANES, LANES), 1), 1.0, 0.0).astype(BF16)
    edge_t[1] = placed(1, 0)
    field_edge[1] = rounded(dot_nt(w_ref[...], edge_t[1, :, 0:C]))

    lane = iota((C, LANES), 1)
    left = lax.rem(lane, 2) == 1
    outer = (lane == 0) | (lane == LANES - 1)
    for j in range(3):
        rows = slice(C * j, C * (j + 1))
        beside = field_edge[1, rows, :]
        along_y = [pltpu.roll(beside, 2, 1), beside, pltpu.roll(beside, LANES - 2, 1)]
        along_z = []
        for a in range(3):
            part = None
            for b in range(3):
                tap = 9 * a + 3 * b
                term = jnp.where(left, weights[tap, rows, :], weights[tap + 2, rows, :]) * along_y[b]
                part = term if part is None else part + term
            along_z.append(part)
        part = along_z[1] + (pltpu.roll(along_z[0], 12, 1) + pltpu.roll(along_z[2], LANES - 12, 1))
        for y in range(2):
            for z in range(4):
                value = partial[y, z, rows, :] + jnp.where(outer, turned(part, z, y), 0.0)
                mixed[y + 1, z, rows, :] = value.astype(BF16)

    row, lane = iota((C, LANES), 0), iota((C, LANES), 1)
    upper = row < HEAD
    gram = jnp.zeros((C, LANES), F32)
    value = jnp.zeros((C, LANES), F32)
    square_q = jnp.zeros((C, LANES), F32)
    square_k = jnp.zeros((C, LANES), F32)
    for y in range(2):
        for z in range(4):
            q, k = mixed[y + 1, z, 0:C, :], mixed[y + 1, z, C : 2 * C, :]
            gram = gram + dot_nt(q, mixed[y + 1, z, C : C + LANES, :])
            value = value + dot_nt(g_ref[y, z], mixed[y + 1, z, C3 - LANES : C3, :])
            square_q = square_q + jnp.square(q.astype(F32))
            square_k = square_k + jnp.square(k.astype(F32))
    gram = jnp.where(upper, gram, pltpu.roll(gram, LANES - HEAD, 1))
    value = jnp.where(upper, pltpu.roll(value, 16, 1), pltpu.roll(value, LANES - 32, 1))
    sum_q = jnp.sum(square_q, axis=1, keepdims=True)
    sum_k = jnp.sum(square_k, axis=1, keepdims=True)
    pay1[...] = jnp.where(
        lane < HEAD,
        gram,
        jnp.where(lane < 2 * HEAD, value, jnp.where(lane == C, sum_q, jnp.where(lane == C + 1, sum_k, 0.0))),
    )
    rows1 = C // n_bulk
    for i in range(n_bulk):
        pack1[i] = pay1[rows1 * i : rows1 * (i + 1), :]
    first.start()

    make_messages(1)
    send_edges(1)
    wait_row(1)
    edge_x[...] = dot_nt(eye, edge_t[1]).astype(BF16)
    make_field((-2, 3), True)
    for y in range(-1, 3):
        for z in range(4):
            edge = turned(field_edge[1].astype(BF16), z, y).astype(F32)
            field[0, y + 2, z, :, 0:1] = edge[:, 0:1]
            field[2, y + 2, z, :, LANES - 1 : LANES] = edge[:, LANES - 1 : LANES]
    for c in (0, 2):
        edge_t[c] = placed(c, 0)
        field_edge[c] = rounded(dot_nt(w_ref[...], edge_t[c, :, 0:C]))
    for j in range(3):
        rows = slice(C * j, C * (j + 1))
        along_z = []
        for a in range(3):
            along_y = []
            for b in range(3):
                part = None
                for c in range(3):
                    term = weights[9 * a + 3 * b + c, rows, :] * field_edge[c, rows, :]
                    part = term if part is None else part + term
                along_y.append(part)
            along_z.append(
                along_y[1] + (pltpu.roll(along_y[0], 2, 1) + pltpu.roll(along_y[2], LANES - 2, 1))
            )
        part = along_z[1] + (pltpu.roll(along_z[0], 12, 1) + pltpu.roll(along_z[2], LANES - 12, 1))
        mixed_edge[rows, :] = part.astype(BF16)
    first.middle()
    make_mixed(-1)
    make_mixed(2)
    first.final()
    wait_row(2)
    wait_edges(1)
    edge_t[3] = placed(1, 1)
    edge_g[...] = dot_nt(eye, edge_t[3]).astype(BF16)
    first.finish()

    for i in range(n_bulk):
        pay1[rows1 * i : rows1 * (i + 1), :] = whole1[i]
    sums = pay1[...]
    value = pltpu.roll(sums, LANES - HEAD, 1)
    inv_q = 1.0 / jnp.sqrt(sums[:, C : C + 1] + 1e-06)
    inv_k = 1.0 / jnp.sqrt(sums[:, C + 1 : C + 2] + 1e-06)
    inv_k0 = jnp.sum(jnp.where(row == lane, inv_k, 0.0), axis=0, keepdims=True)
    inv_k1 = jnp.sum(jnp.where(row == lane + HEAD, inv_k, 0.0), axis=0, keepdims=True)
    inv_kr = jnp.where(upper, inv_k0, inv_k1)
    inner = lane < HEAD
    sharp = jnp.where(upper, sharp_ref[0], sharp_ref[1])
    cosine = jnp.where(inner, sums * inv_q * inv_kr, 0.0)
    numerators = jnp.where(inner, jnp.exp(sharp * cosine), 0.0)
    attention = numerators / jnp.sum(numerators, axis=1, keepdims=True)
    score = attention * (value - jnp.sum(attention * value, axis=1, keepdims=True))
    by_cosine = score * cosine
    pay1[...] = by_cosine
    cosine_grad = sharp * score
    diagonal = cosine_grad * cosine
    diag_q = jnp.sum(diagonal, axis=1, keepdims=True)
    coupling = rounded(inv_q * cosine_grad * inv_kr)

    def blocks(v):
        return jnp.where(
            upper, jnp.where(inner, v, 0.0), jnp.where((lane >= HEAD) & (lane < C), pltpu.roll(v, HEAD, 1), 0.0)
        )

    def transposed(k, v):
        turn[k, 0:C, :] = v
        turn[k, C:LANES, :] = jnp.zeros((LANES - C, LANES), F32)
        return turn[k].T

    coupled = blocks(coupling)
    couple[0] = coupled.astype(BF16)
    couple[1] = transposed(0, coupled)[0:C, :].astype(BF16)
    couple[2] = transposed(1, blocks(attention))[0:C, :].astype(BF16)
    diag_k = jnp.sum(transposed(2, blocks(diagonal)), axis=1, keepdims=True)[0:C, :]
    coef[0] = jnp.broadcast_to(inv_q * inv_q * diag_q, (C, LANES))
    coef[1] = jnp.broadcast_to(inv_k * inv_k * diag_k, (C, LANES))

    def gradients(q, k, g):
        grad_q = dot(couple[0, :, 0:C], k) - coef[0] * q.astype(F32)
        grad_k = dot(couple[1, :, 0:C], q) - coef[1] * k.astype(F32)
        return grad_q, grad_k, dot(couple[2, :, 0:C], g)

    def flag(condition):
        return jnp.where(condition, 1.0, 0.0)

    mask = (
        flags_ref[0:1, :]
        * (1.0 - flags_ref[1:2, :] * flag(col == 0))
        * (1.0 - flags_ref[2:3, :] * flag(col == n_col - 1))
        * (1.0 - flags_ref[3:4, :] * flag(bulk == 0))
        * (1.0 - flags_ref[4:5, :] * flag(bulk == n_bulk - 1))
    )
    edges = gradients(mixed_edge[0:C, :], mixed_edge[C : 2 * C, :], edge_g[0:C, :])
    for part in range(3):
        grads_edge[C * part : C * (part + 1), :] = jnp.where(mask > 0.5, edges[part], 0.0).astype(BF16)

    def grad_planes(z):
        for y in range(-1, 3):
            g = g_ref[y, z] if y in (0, 1) else gh[0 if y == -1 else 1, z]
            made = gradients(mixed[y + 1, z, 0:C, :], mixed[y + 1, z, C : 2 * C, :], g)
            for part in range(3):
                rows = slice(C * part, C * (part + 1))
                plane = rounded(made[part])
                if y == -1:
                    plane = plane * flag(low)
                if y == 2:
                    plane = plane * flag(high)
                edge = turned(grads_edge[rows, :], z, y).astype(F32)
                narrow = plane.astype(BF16)
                before = jnp.where(lane == 0, edge, pltpu.roll(narrow, 1, 1).astype(F32))
                after = jnp.where(lane == LANES - 1, edge, pltpu.roll(narrow, LANES - 1, 1).astype(F32))
                grads[0, y + 1, z, rows, :] = before
                grads[1, y + 1, z, rows, :] = plane
                grads[2, y + 1, z, rows, :] = after

    for z in range(4):
        grad_planes(z)

    for y in range(2):

        def sink(z, rows, value, y=y):
            field_grad[y, z, rows, :] = value.astype(BF16)

        conv(grads, y, weights, True, sink)

    def depth(j, carry):
        group = pl.ds(pl.multiple_of(j * DEPTH_CHUNK, DEPTH_CHUNK), DEPTH_CHUNK)
        weight = jnp.zeros((DEPTH_CHUNK, C), F32)
        for y in range(2):
            for z in range(4):
                weight = weight + dot_nt(field_grad[y, z, group, :], x_ref[y, z])
        lane = iota((16, LANES), 1)
        for h in range(DEPTH_CHUNK // 16):
            rows = pl.ds(pl.multiple_of(j * DEPTH_CHUNK + 16 * h, 16), 16)
            made = jnp.zeros((16, LANES), F32)
            mine = [[grads[1, y + 1, z, rows, :] for z in range(4)] for y in range(2)]
            for b in range(3):
                for c in range(3):
                    cells = [[field[c, y + b + 1, z, rows, :] for z in range(4)] for y in range(2)]
                    for a in range(3):
                        total = None
                        for y in range(2):
                            for z in range(4):
                                if 0 <= z + a - 1 < 4:
                                    term = mine[y][z] * cells[y][z + a - 1]
                                    total = term if total is None else total + term
                        tap = 9 * a + 3 * b + c
                        made = jnp.where(lane == C + tap, jnp.sum(total, axis=1, keepdims=True), made)
            pay2[rows, :] = made
        pay2[group, 0:C] = weight
        return carry

    lax.fori_loop(0, C3 // DEPTH_CHUNK, depth, 0)
    rows2 = C3 // n_bulk
    for i in range(n_bulk):
        pack2[i] = pay2[rows2 * i : rows2 * (i + 1), :]
    second.start()

    by_cosine = pay1[...]
    for e in range(2):
        total = jnp.sum(jnp.where(upper if e == 0 else ~upper, by_cosine, 0.0), axis=1, keepdims=True)
        kd_ref[27 + e : 28 + e, :] = jnp.broadcast_to(jnp.sum(total, axis=0, keepdims=True) * scale, (1, C3))
    for z in range(4):
        rows_y = [dot_tn(w_ref[...], field_grad[y, z]) for y in range(2)]
        dx_ref[:, z] = jnp.stack(rows_y, axis=1).astype(BF16)
    for k in range(3):
        pl.when(high)(lambda k=k: row_copy(k, True).wait_send())
        pl.when(low)(lambda k=k: row_copy(k, False).wait_send())
    for kind in range(2):
        for (a, b) in around:
            pl.when(inside(a, b))(lambda a=a, b=b, kind=kind: edge_copy(kind, a, b).wait_send())
    first.drain()
    second.middle()
    second.final()
    second.finish()
    for i in range(n_bulk):
        pay2[rows2 * i : rows2 * (i + 1), :] = whole2[i]
    pd_ref[...] = pay2[:, 0:C] * scale
    taps_c[0:C3, :] = pay2[...] * scale
    for j in range(3):
        taps_t[:, LANES * j : LANES * (j + 1)] = taps_c[LANES * j : LANES * (j + 1), :].T
    kd_ref[0:27, :] = taps_t[C : C + 27, 0:C3]
    second.drain()


def hand_out(dx_in, pd_in, kd_in, dx_ref, pd_ref, kd_ref, sd_ref):
    dx_ref[...] = dx_in[...]
    pd_ref[...] = pd_in[...]
    kd_ref[...] = kd_in[0:27, :]
    for e in range(2):
        sd_ref[e] = kd_in[27 + e, 0]


def local(x, g, w, k, sharp):
    n_col, n_bulk = lax.axis_size("col"), lax.axis_size("bulk")
    scale = 1.0 / math.sqrt(x.shape[1] * x.shape[2] * x.shape[3] * n_col * n_bulk)
    place, flags = edge_tables()
    vmem = pl.BlockSpec(memory_space=pltpu.VMEM)
    smem = pl.BlockSpec(memory_space=pltpu.SMEM)
    hbm = pl.BlockSpec(memory_space=pl.ANY)
    rows1, rows2 = C // n_bulk, C3 // n_bulk

    def reduction(rows):
        return [
            pltpu.VMEM((n_bulk, rows, LANES), F32),
            pltpu.VMEM((n_bulk, rows, LANES), F32),
            pltpu.VMEM((n_col, rows, LANES), F32),
            pltpu.VMEM((n_bulk, rows, LANES), F32),
        ]

    def dma(count):
        return pltpu.SemaphoreType.DMA((count,))

    reduction_sems = [pltpu.SemaphoreType.DMA] * 6
    dx, pd, kd = pl.pallas_call(
        functools.partial(kernel, (n_col, n_bulk), scale),
        out_shape=(
            pltpu.VMEM((C, 4, 2, LANES), BF16),
            pltpu.VMEM((C3, C), F32),
            pltpu.VMEM((32, C3), F32),
        ),
        in_specs=[hbm, hbm, hbm, hbm, smem, hbm, vmem],
        out_specs=(vmem, vmem, vmem),
        scratch_shapes=[
            pltpu.VMEM(x.shape, BF16),
            pltpu.VMEM(g.shape, BF16),
            pltpu.VMEM(w.shape, BF16),
            pltpu.VMEM((27, C3), F32),
            pltpu.VMEM(place.shape, BF16),
            pltpu.SemaphoreType.DMA((5,)),
            pltpu.VMEM((2, 4, C, LANES), BF16),
            pltpu.VMEM((2, 4, C, LANES), BF16),
            pltpu.VMEM((4, 4, C, LANES), BF16),
            pltpu.VMEM((2, 4, C, LANES), BF16),
            pltpu.VMEM((2, 32, LANES), BF16),
            pltpu.VMEM((2, 9, 32, LANES), BF16),
            pltpu.VMEM((4, LANES, LANES), BF16),
            pltpu.VMEM((LANES, LANES), BF16),
            pltpu.VMEM((LANES, LANES), BF16),
            pltpu.VMEM((LANES, 3 * LANES), F32),
            pltpu.VMEM((3 * LANES, LANES), F32),
            pltpu.VMEM((27, C3, LANES), F32),
            pltpu.VMEM((3, 6, 4, C3, LANES), F32),
            pltpu.VMEM((3, C3, LANES), F32),
            pltpu.VMEM((4, 4, C3, LANES), BF16),
            pltpu.VMEM((C3, LANES), BF16),
            pltpu.VMEM((3, 4, 4, C3, LANES), F32),
            pltpu.VMEM((C3, LANES), BF16),
            pltpu.VMEM((2, 4, C3, LANES), BF16),
            pltpu.VMEM((3, LANES, LANES), F32),
            pltpu.VMEM((2, 4, C3, LANES), F32),
            pltpu.VMEM((3, C, LANES), BF16),
            pltpu.VMEM((2, C, LANES), F32),
            pltpu.VMEM((C, LANES), F32),
            pltpu.VMEM((C3, LANES), F32),
        ]
        + reduction(rows1)
        + reduction(rows2)
        + [dma(6), dma(6), dma(18), dma(18)]
        + reduction_sems
        + reduction_sems,
        compiler_params=pltpu.CompilerParams(
            collective_id=0, has_side_effects=True, vmem_limit_bytes=56 * 2**20
        ),
    )(
        x,
        g,
        w,
        k.T,
        sharp,
        jnp.asarray(place, BF16),
        jnp.asarray(flags),
    )
    dx, pd, kd, sd = pl.pallas_call(
        hand_out,
        out_shape=(
            jax.ShapeDtypeStruct((C, 4, 2, LANES), BF16),
            jax.ShapeDtypeStruct((C3, C), F32),
            jax.ShapeDtypeStruct((27, C3), F32),
            jax.ShapeDtypeStruct((2,), F32),
        ),
        in_specs=[vmem, vmem, vmem],
        out_specs=(vmem, vmem, vmem, smem),
        compiler_params=pltpu.CompilerParams(vmem_limit_bytes=4 * 2**20),
    )(dx, pd, kd)
    return dx, pd, kd.T, sd


def solution(mesh):
    return jax.shard_map(
        local,
        mesh=mesh,
        in_specs=(P(None, None, "bulk", "col"), P(None, None, "bulk", "col"), P(), P(), P()),
        out_specs=(P(None, None, "bulk", "col"), P(), P(), P()),
        check_vma=False,
    )
```

```python
import functools
import math

import jax
import jax.numpy as jnp
import numpy as np
from jax import lax
from jax.experimental import pallas as pl
from jax.experimental.pallas import tpu as pltpu
from jax.sharding import PartitionSpec as P

MESH = pl.DeviceIdType.MESH
F32 = jnp.float32
BF16 = jnp.bfloat16
C = 96
HEAD = 48
C3 = 3 * C
LANES = 128
CHUNK = 32
DEPTH_CHUNK = 96
EARLY_TAPS = 10
EDGE_COLUMNS = (0, 1, LANES - 2, LANES - 1)
NEIGHBOURS = [(a, b) for a in (-1, 0, 1) for b in (-1, 0, 1)]


def slot_of(a, b):
    return 3 * (a + 1) + b + 1


def edge_index(z, y):
    return (z + 1) * 6 + y + 2


def edge_tables():
    place = np.zeros((3, LANES, 9 * 32), np.float32)
    flags = np.zeros((8, LANES), np.float32)
    for (a, b) in NEIGHBOURS:
        for s, column in enumerate(EDGE_COLUMNS):
            x = LANES * a + column
            for y in range(2):
                for z in range(4):
                    k = slot_of(a, b) * 32 + s * 8 + y * 4 + z
                    index = 2 * edge_index(z, 2 * b + y)
                    for c in (-1, 0, 1):
                        if x == -1 + c:
                            place[c + 1, index + 1, k] = 1.0
                        if x == LANES + c:
                            place[c + 1, index, k] = 1.0
    for z in range(4):
        for y in range(-1, 3):
            for left in range(2):
                lane = 2 * edge_index(z, y) + left
                flags[0, lane] = 1.0
                flags[1, lane] = left
                flags[2, lane] = 1 - left
                flags[3, lane] = y == -1
                flags[4, lane] = y == 2
    return place.reshape(3 * LANES, 9 * 32), flags


def dot_nt(a, b):
    return lax.dot_general(a, b, (((1,), (1,)), ((), ())), preferred_element_type=F32)


def dot_tn(a, b):
    return lax.dot_general(a, b, (((0,), (0,)), ((), ())), preferred_element_type=F32)


def dot(a, b):
    return jnp.dot(a, b, preferred_element_type=F32)


def iota(shape, dim):
    return lax.broadcasted_iota(jnp.int32, shape, dim)


def rounded(v):
    return v.astype(BF16).astype(F32)


def remote(src, dst, send, recv, target):
    return pltpu.make_async_remote_copy(
        src_ref=src, dst_ref=dst, send_sem=send, recv_sem=recv, device_id=target, device_id_type=MESH
    )


def ring_distance(step, count):
    return min(step, count - step)


def bulk_peers(bulk, n_bulk):
    if n_bulk != 32:
        return [lax.rem(bulk + step, n_bulk) for step in range(1, n_bulk)]
    ys = [lax.rem(bulk // 8 + d, 4) * 8 for d in range(4)]
    xs = [lax.rem(lax.rem(bulk // 2, 4) + d, 4) * 2 for d in range(4)]
    cores = [lax.rem(bulk + d, 2) for d in range(2)]
    steps = [(y, x, c) for y in range(4) for x in range(4) for c in range(2)][1:]
    steps.sort(key=lambda t: -2 * ring_distance(t[0], 4) - 2 * ring_distance(t[1], 4) - t[2])
    return [ys[y] + xs[x] + cores[c] for y, x, c in steps]


def col_peers(col, n_col):
    steps = sorted(range(1, n_col), key=lambda d: -ring_distance(d, n_col))
    return [lax.rem(col + d, n_col) for d in steps]


class Reduction:
    def __init__(self, place, peers, pack, parts, planes, whole, sems):
        self.col, self.bulk = place
        self.in_plane, self.in_col = peers
        self.pack, self.parts, self.planes, self.whole = pack, parts, planes, whole
        self.s_send, self.s_recv, self.z_send, self.z_recv, self.g_send, self.g_recv = sems

    def scattered(self):
        rest = pl.ds(0, len(self.in_plane))
        target = (self.col, self.in_plane[0])
        return remote(self.pack.at[rest], self.parts.at[rest], self.s_send, self.s_recv, target)

    def crossed(self):
        rest = pl.ds(0, len(self.in_col))
        target = (self.in_col[0], self.bulk)
        return remote(self.planes.at[rest], self.planes.at[rest], self.z_send, self.z_recv, target)

    def gathered(self):
        rest = pl.ds(0, len(self.in_plane))
        target = (self.col, self.in_plane[0])
        return remote(self.whole.at[rest], self.whole.at[rest], self.g_send, self.g_recv, target)

    def start(self):
        for peer in self.in_plane:
            remote(
                self.pack.at[peer], self.parts.at[self.bulk], self.s_send, self.s_recv, (self.col, peer)
            ).start()
        self.parts[self.bulk] = self.pack[self.bulk]

    def middle(self):
        self.scattered().wait_recv()
        self.planes[self.col] = jnp.sum(self.parts[...], axis=0)
        mine = self.planes.at[self.col]
        for peer in self.in_col:
            remote(mine, mine, self.z_send, self.z_recv, (peer, self.bulk)).start()

    def final(self):
        self.crossed().wait_recv()
        self.whole[self.bulk] = jnp.sum(self.planes[...], axis=0)
        mine = self.whole.at[self.bulk]
        for peer in self.in_plane:
            remote(mine, mine, self.g_send, self.g_recv, (self.col, peer)).start()

    def finish(self):
        self.gathered().wait_recv()

    def drain(self):
        self.scattered().wait_send()
        self.crossed().wait_send()
        self.gathered().wait_send()


def conv(source, weights, flip, jobs):
    def chunk(rows, y0, sink, bs=(0, 1, 2), start=None):
        total = [None if start is None else start(z, rows) for z in range(4)]
        for b in bs:
            for c in range(3):
                cells = [source[c, y0 + b, z, rows, :] for z in range(4)]
                for a in range(3):
                    tap = 9 * a + 3 * b + c
                    weight = weights[26 - tap if flip else tap, rows, :]
                    for z in range(4):
                        if 0 <= z + a - 1 < 4:
                            term = weight * cells[z + a - 1]
                            total[z] = term if total[z] is None else total[z] + term
        for z in range(4):
            sink(z, rows, total[z])

    def body(j, carry):
        for h in range(3):
            for job in jobs:
                chunk(pl.ds(pl.multiple_of(j * 3 * CHUNK + h * CHUNK, CHUNK), CHUNK), *job)
        return carry

    lax.fori_loop(0, C3 // (3 * CHUNK), body, 0)


def kernel(
    sizes,
    scale,
    x_hbm,
    g_hbm,
    w_hbm,
    k_hbm,
    sharp_ref,
    place_hbm,
    flags_ref,
    dx_ref,
    pd_ref,
    kd_ref,
    x_in,
    g_in,
    w_ref,
    k_ref,
    place_ref,
    load_sem,
    x_ref,
    g_ref,
    xh,
    gh,
    messages,
    arrived,
    edge_t,
    edge_x,
    edge_g,
    taps_t,
    taps_c,
    weights,
    field,
    field_edge,
    mixed,
    mixed_edge,
    grads,
    grads_edge,
    field_grad,
    turn,
    partial,
    couple,
    coef,
    pay1,
    pay2,
    pack1,
    parts1,
    planes1,
    whole1,
    pack2,
    parts2,
    planes2,
    whole2,
    row_send,
    row_recv,
    edge_send,
    edge_recv,
    *sems,
):
    n_col, n_bulk = sizes
    col, bulk = lax.axis_index("col"), lax.axis_index("bulk")
    peers = bulk_peers(bulk, n_bulk), col_peers(col, n_col)
    first = Reduction((col, bulk), peers, pack1, parts1, planes1, whole1, sems[:6])
    second = Reduction((col, bulk), peers, pack2, parts2, planes2, whole2, sems[6:])
    low, high = bulk > 0, bulk < n_bulk - 1

    loads = [
        pltpu.make_async_copy(source, target, load_sem.at[i])
        for i, (source, target) in enumerate(
            ((x_hbm, x_in), (g_hbm, g_in), (w_hbm, w_ref), (k_hbm, k_ref), (place_hbm, place_ref))
        )
    ]
    for i in (3, 0, 2, 1, 4):
        loads[i].start()

    xh[...] = jnp.zeros_like(xh)
    gh[...] = jnp.zeros_like(gh)
    arrived[...] = jnp.zeros_like(arrived)
    barrier = pltpu.get_barrier_semaphore()

    def greet(target):
        pl.semaphore_signal(barrier, inc=1, device_id=target, device_id_type=MESH)

    for peer in peers[0][:10]:
        greet((col, peer))
    for peer in peers[1]:
        greet((peer, bulk))
    for a in (1, n_col - 1):
        for b in (1, n_bulk - 1):
            greet((lax.rem(col + a, n_col), lax.rem(bulk + b, n_bulk)))
    for peer in peers[0][10:]:
        greet((col, peer))
    loads[3].wait()
    taps_t[...] = jnp.zeros_like(taps_t)
    taps_t[0:27, 0:C3] = k_ref[...]
    for j in range(3):
        taps_c[LANES * j : LANES * (j + 1), :] = taps_t[:, LANES * j : LANES * (j + 1)].T

    def spread_taps(which):
        for t in which:
            weights[t] = jnp.broadcast_to(taps_c[0:C3, t : t + 1], (C3, LANES))

    spread_taps(range(EARLY_TAPS))
    row32, lane32 = iota((32, LANES), 0), iota((32, LANES), 1)

    def take_in(kind):
        source, planes = (x_in, g_in)[kind], (x_ref, g_ref)[kind]
        loads[kind].wait()
        for z in range(4):
            pair = source[:, z].astype(F32)
            for y in range(2):
                planes[y, z] = pair[:, y, :].astype(BF16)

    def make_messages(kind):
        planes = (x_ref, g_ref)[kind]
        total = jnp.zeros((32, C), F32)
        for y in range(2):
            for z in range(4):
                pick = jnp.zeros((32, LANES), jnp.bool_)
                for s, column in enumerate(EDGE_COLUMNS):
                    pick = pick | ((row32 == s * 8 + y * 4 + z) & (lane32 == column))
                total = total + dot_nt(jnp.where(pick, 1.0, 0.0).astype(BF16), planes[y, z])
        messages[kind] = jnp.zeros((32, LANES), BF16)
        messages[kind, :, 0:C] = total.astype(BF16)

    take_in(0)
    make_messages(0)

    pl.semaphore_wait(barrier, n_bulk + n_col - 2 + 4)

    def row_copy(k, down):
        y = 1 if down == (k != 1) else 0
        if k == 2:
            source, target = g_ref.at[y], gh.at[0 if down else 1]
        else:
            source, target = x_ref.at[y], xh.at[(1, 0)[k] if down else (2, 3)[k]]
        sem = 2 * k + (1 if down else 0)
        return remote(source, target, row_send.at[sem], row_recv.at[sem], (col, lax.rem(bulk + (1 if down else n_bulk - 1), n_bulk)))

    def edge_copy(kind, a, b):
        slot = slot_of(-a, -b)
        target = (lax.rem(col + a + n_col, n_col), lax.rem(bulk + b + n_bulk, n_bulk))
        sem = 9 * kind + slot
        return remote(messages.at[kind], arrived.at[kind, slot], edge_send.at[sem], edge_recv.at[sem], target)

    def inside(a, b):
        return (col + a >= 0) & (col + a < n_col) & (bulk + b >= 0) & (bulk + b < n_bulk)

    around = [(a, b) for (a, b) in NEIGHBOURS if (a, b) != (0, 0)]
    around.sort(key=lambda t: -abs(t[0]) - abs(t[1]))

    def send_edges(kind):
        for (a, b) in around:
            pl.when(inside(a, b))(lambda a=a, b=b: edge_copy(kind, a, b).start())
        arrived[kind, slot_of(0, 0)] = messages[kind]

    def wait_edges(kind):
        for (a, b) in around:
            pl.when(inside(a, b))(lambda a=a, b=b: edge_copy(kind, -a, -b).wait_recv())

    def send_row(k):
        pl.when(high)(lambda: row_copy(k, True).start())
        pl.when(low)(lambda: row_copy(k, False).start())

    send_edges(0)
    send_row(0)

    def wait_row(k):
        pl.when(low)(lambda: row_copy(k, True).wait_recv())
        pl.when(high)(lambda: row_copy(k, False).wait_recv())

    def turned(values, z, y):
        return pltpu.roll(values, LANES - 1 - 2 * edge_index(z, y), 1)

    def shifted(values, edge):
        lane = iota(values.shape, 1)
        before = jnp.where(lane == 0, edge, pltpu.roll(values, 1, 1).astype(F32))
        after = jnp.where(lane == LANES - 1, edge, pltpu.roll(values, LANES - 1, 1).astype(F32))
        return before, after

    def input_row(y):
        return x_ref.at[y] if y in (0, 1) else xh.at[{-2: 0, -1: 1, 2: 2, 3: 3}[y]]

    def make_field(ys, edged):
        for y in ys:
            for z in range(4):
                plane = input_row(y)[z]
                edge = turned(edge_x[0:C, :], z, y).astype(F32) if edged else 0.0
                before, after = shifted(plane, edge)
                cells = jnp.concatenate([before.astype(BF16), plane, after.astype(BF16)], axis=1)
                made = rounded(dot(w_ref[...], cells))
                for c in range(3):
                    field[c, y + 2, z] = made[:, LANES * c : LANES * (c + 1)]

    def gather(parts):
        def job(y, bs, start):
            def sink(z, rows, value):
                partial[y, z, rows, :] = value

            return y + 1, sink, bs, start

        conv(field, weights, False, [job(*part) for part in parts])

    def make_mixed(ys):
        def job(y):
            def sink(z, rows, value):
                mixed[y + 1, z, rows, :] = value.astype(BF16)

            return y + 1, sink

        conv(field, weights, False, [job(y) for y in ys])

    for load in (loads[2], loads[4]):
        load.wait()
    spread_taps(range(EARLY_TAPS, 27))

    make_field((0, 1), False)
    gather([(0, (1, 2), None), (1, (0, 1), None)])
    take_in(1)
    wait_row(0)
    for k in (1, 2):
        send_row(k)
    make_field((-1, 2), False)
    gather(
        [
            (0, (0,), lambda z, rows: partial[0, z, rows, :]),
            (1, (2,), lambda z, rows: partial[1, z, rows, :]),
        ]
    )
    wait_edges(0)

    def placed(c, kind):
        return dot(place_ref[LANES * c : LANES * (c + 1), :], arrived[kind].reshape(9 * 32, LANES)).astype(BF16)

    eye = jnp.where(iota((LANES, LANES), 0) == iota((LANES, LANES), 1), 1.0, 0.0).astype(BF16)
    edge_t[1] = placed(1, 0)
    field_edge[1] = rounded(dot_nt(w_ref[...], edge_t[1, :, 0:C]))

    lane = iota((C, LANES), 1)
    left = lax.rem(lane, 2) == 1
    outer = (lane == 0) | (lane == LANES - 1)
    for j in range(3):
        rows = slice(C * j, C * (j + 1))
        beside = field_edge[1, rows, :]
        narrow = beside.astype(BF16)
        along_y = [pltpu.roll(narrow, 2, 1).astype(F32), beside, pltpu.roll(narrow, LANES - 2, 1).astype(F32)]
        along_z = []
        for a in range(3):
            part = None
            for b in range(3):
                tap = 9 * a + 3 * b
                term = jnp.where(left, weights[tap, rows, :], weights[tap + 2, rows, :]) * along_y[b]
                part = term if part is None else part + term
            along_z.append(part)
        part = along_z[1] + (pltpu.roll(along_z[0], 12, 1) + pltpu.roll(along_z[2], LANES - 12, 1))
        for y in range(2):
            for z in range(4):
                value = partial[y, z, rows, :] + jnp.where(outer, turned(part, z, y), 0.0)
                mixed[y + 1, z, rows, :] = value.astype(BF16)

    row, lane = iota((C, LANES), 0), iota((C, LANES), 1)
    upper = row < HEAD
    gram = jnp.zeros((C, LANES), F32)
    value = jnp.zeros((C, LANES), F32)
    square_q = jnp.zeros((C, LANES), F32)
    square_k = jnp.zeros((C, LANES), F32)
    for y in range(2):
        for z in range(4):
            q, k = mixed[y + 1, z, 0:C, :], mixed[y + 1, z, C : 2 * C, :]
            gram = gram + dot_nt(q, mixed[y + 1, z, C : C + LANES, :])
            value = value + dot_nt(g_ref[y, z], mixed[y + 1, z, C3 - LANES : C3, :])
            square_q = square_q + jnp.square(q.astype(F32))
            square_k = square_k + jnp.square(k.astype(F32))
    gram = jnp.where(upper, gram, pltpu.roll(gram, LANES - HEAD, 1))
    value = jnp.where(upper, pltpu.roll(value, 16, 1), pltpu.roll(value, LANES - 32, 1))
    sum_q = jnp.sum(square_q, axis=1, keepdims=True)
    sum_k = jnp.sum(square_k, axis=1, keepdims=True)
    pay1[...] = jnp.where(
        lane < HEAD,
        gram,
        jnp.where(lane < 2 * HEAD, value, jnp.where(lane == C, sum_q, jnp.where(lane == C + 1, sum_k, 0.0))),
    )
    rows1 = C // n_bulk
    for i in range(n_bulk):
        pack1[i] = pay1[rows1 * i : rows1 * (i + 1), :]
    first.start()

    make_messages(1)
    send_edges(1)
    wait_row(1)
    edge_x[...] = dot_nt(eye, edge_t[1]).astype(BF16)
    make_field((-2, 3), True)
    for y in range(-1, 3):
        for z in range(4):
            edge = turned(field_edge[1].astype(BF16), z, y).astype(F32)
            field[0, y + 2, z, :, 0:1] = edge[:, 0:1]
            field[2, y + 2, z, :, LANES - 1 : LANES] = edge[:, LANES - 1 : LANES]
    for c in (0, 2):
        edge_t[c] = placed(c, 0)
        field_edge[c] = rounded(dot_nt(w_ref[...], edge_t[c, :, 0:C]))
    for j in range(3):
        rows = slice(C * j, C * (j + 1))
        along_z = []
        for a in range(3):
            along_y = []
            for b in range(3):
                part = None
                for c in range(3):
                    term = weights[9 * a + 3 * b + c, rows, :] * field_edge[c, rows, :]
                    part = term if part is None else part + term
                along_y.append(part)
            along_z.append(
                along_y[1] + (pltpu.roll(along_y[0], 2, 1) + pltpu.roll(along_y[2], LANES - 2, 1))
            )
        part = along_z[1] + (pltpu.roll(along_z[0], 12, 1) + pltpu.roll(along_z[2], LANES - 12, 1))
        mixed_edge[rows, :] = part.astype(BF16)
    first.middle()
    make_mixed((-1, 2))
    first.final()
    wait_row(2)
    wait_edges(1)
    edge_t[3] = placed(1, 1)
    edge_g[...] = dot_nt(eye, edge_t[3]).astype(BF16)
    first.finish()

    for i in range(n_bulk):
        pay1[rows1 * i : rows1 * (i + 1), :] = whole1[i]
    sums = pay1[...]
    value = pltpu.roll(sums, LANES - HEAD, 1)
    inv_q = 1.0 / jnp.sqrt(sums[:, C : C + 1] + 1e-06)
    inv_k = 1.0 / jnp.sqrt(sums[:, C + 1 : C + 2] + 1e-06)
    inv_k0 = jnp.sum(jnp.where(row == lane, inv_k, 0.0), axis=0, keepdims=True)
    inv_k1 = jnp.sum(jnp.where(row == lane + HEAD, inv_k, 0.0), axis=0, keepdims=True)
    inv_kr = jnp.where(upper, inv_k0, inv_k1)
    inner = lane < HEAD
    sharp = jnp.where(upper, sharp_ref[0], sharp_ref[1])
    cosine = jnp.where(inner, sums * inv_q * inv_kr, 0.0)
    numerators = jnp.where(inner, jnp.exp(sharp * cosine), 0.0)
    attention = numerators / jnp.sum(numerators, axis=1, keepdims=True)
    score = attention * (value - jnp.sum(attention * value, axis=1, keepdims=True))
    by_cosine = score * cosine
    pay1[...] = by_cosine
    cosine_grad = sharp * score
    diagonal = cosine_grad * cosine
    diag_q = jnp.sum(diagonal, axis=1, keepdims=True)
    coupling = rounded(inv_q * cosine_grad * inv_kr)

    def blocks(v):
        return jnp.where(
            upper, jnp.where(inner, v, 0.0), jnp.where((lane >= HEAD) & (lane < C), pltpu.roll(v, HEAD, 1), 0.0)
        )

    def transposed(k, v):
        turn[k, 0:C, :] = v
        turn[k, C:LANES, :] = jnp.zeros((LANES - C, LANES), F32)
        return turn[k].T

    coupled = blocks(coupling)
    couple[0] = coupled.astype(BF16)
    couple[1] = transposed(0, coupled)[0:C, :].astype(BF16)
    couple[2] = transposed(1, blocks(attention))[0:C, :].astype(BF16)
    diag_k = jnp.sum(transposed(2, blocks(diagonal)), axis=1, keepdims=True)[0:C, :]
    coef[0] = jnp.broadcast_to(inv_q * inv_q * diag_q, (C, LANES))
    coef[1] = jnp.broadcast_to(inv_k * inv_k * diag_k, (C, LANES))

    def gradients(q, k, g):
        grad_q = dot(couple[0, :, 0:C], k) - coef[0] * q.astype(F32)
        grad_k = dot(couple[1, :, 0:C], q) - coef[1] * k.astype(F32)
        return grad_q, grad_k, dot(couple[2, :, 0:C], g)

    def flag(condition):
        return jnp.where(condition, 1.0, 0.0)

    mask = (
        flags_ref[0:1, :]
        * (1.0 - flags_ref[1:2, :] * flag(col == 0))
        * (1.0 - flags_ref[2:3, :] * flag(col == n_col - 1))
        * (1.0 - flags_ref[3:4, :] * flag(bulk == 0))
        * (1.0 - flags_ref[4:5, :] * flag(bulk == n_bulk - 1))
    )
    edges = gradients(mixed_edge[0:C, :], mixed_edge[C : 2 * C, :], edge_g[0:C, :])
    for part in range(3):
        grads_edge[C * part : C * (part + 1), :] = jnp.where(mask > 0.5, edges[part], 0.0).astype(BF16)

    def grad_planes(z):
        for y in range(-1, 3):
            g = g_ref[y, z] if y in (0, 1) else gh[0 if y == -1 else 1, z]
            made = gradients(mixed[y + 1, z, 0:C, :], mixed[y + 1, z, C : 2 * C, :], g)
            for part in range(3):
                rows = slice(C * part, C * (part + 1))
                plane = rounded(made[part])
                if y == -1:
                    plane = plane * flag(low)
                if y == 2:
                    plane = plane * flag(high)
                edge = turned(grads_edge[rows, :], z, y).astype(F32)
                narrow = plane.astype(BF16)
                before = jnp.where(lane == 0, edge, pltpu.roll(narrow, 1, 1).astype(F32))
                after = jnp.where(lane == LANES - 1, edge, pltpu.roll(narrow, LANES - 1, 1).astype(F32))
                grads[0, y + 1, z, rows, :] = before
                grads[1, y + 1, z, rows, :] = plane
                grads[2, y + 1, z, rows, :] = after

    for z in range(4):
        grad_planes(z)

    def spread(y):
        def sink(z, rows, value):
            field_grad[y, z, rows, :] = value.astype(BF16)

        return y, sink

    conv(grads, weights, True, [spread(y) for y in range(2)])

    def depth(j, carry):
        group = pl.ds(pl.multiple_of(j * DEPTH_CHUNK, DEPTH_CHUNK), DEPTH_CHUNK)
        weight = jnp.zeros((DEPTH_CHUNK, C), F32)
        for y in range(2):
            for z in range(4):
                weight = weight + dot_nt(field_grad[y, z, group, :], x_ref[y, z])
        lane = iota((16, LANES), 1)
        for h in range(DEPTH_CHUNK // 16):
            rows = pl.ds(pl.multiple_of(j * DEPTH_CHUNK + 16 * h, 16), 16)
            made = jnp.zeros((16, LANES), F32)
            mine = [[grads[1, y + 1, z, rows, :] for z in range(4)] for y in range(2)]
            for b in range(3):
                for c in range(3):
                    cells = [[field[c, y + b + 1, z, rows, :] for z in range(4)] for y in range(2)]
                    for a in range(3):
                        total = None
                        for y in range(2):
                            for z in range(4):
                                if 0 <= z + a - 1 < 4:
                                    term = mine[y][z] * cells[y][z + a - 1]
                                    total = term if total is None else total + term
                        tap = 9 * a + 3 * b + c
                        made = jnp.where(lane == C + tap, jnp.sum(total, axis=1, keepdims=True), made)
            pay2[rows, :] = made
        pay2[group, 0:C] = weight
        return carry

    lax.fori_loop(0, C3 // DEPTH_CHUNK, depth, 0)
    rows2 = C3 // n_bulk
    for i in range(n_bulk):
        pack2[i] = pay2[rows2 * i : rows2 * (i + 1), :]
    second.start()

    by_cosine = pay1[...]
    for e in range(2):
        total = jnp.sum(jnp.where(upper if e == 0 else ~upper, by_cosine, 0.0), axis=1, keepdims=True)
        kd_ref[27 + e : 28 + e, :] = jnp.broadcast_to(jnp.sum(total, axis=0, keepdims=True) * scale, (1, C3))
    for z in range(4):
        rows_y = [dot_tn(w_ref[...], field_grad[y, z]) for y in range(2)]
        dx_ref[:, z] = jnp.stack(rows_y, axis=1).astype(BF16)
    for k in range(3):
        pl.when(high)(lambda k=k: row_copy(k, True).wait_send())
        pl.when(low)(lambda k=k: row_copy(k, False).wait_send())
    for kind in range(2):
        for (a, b) in around:
            pl.when(inside(a, b))(lambda a=a, b=b, kind=kind: edge_copy(kind, a, b).wait_send())
    first.drain()
    second.middle()
    second.final()
    second.finish()
    for i in range(n_bulk):
        pay2[rows2 * i : rows2 * (i + 1), :] = whole2[i]
    pd_ref[...] = pay2[:, 0:C] * scale
    taps_c[0:C3, :] = pay2[...] * scale
    for j in range(3):
        taps_t[:, LANES * j : LANES * (j + 1)] = taps_c[LANES * j : LANES * (j + 1), :].T
    kd_ref[0:27, :] = taps_t[C : C + 27, 0:C3]
    second.drain()


def hand_out(dx_in, pd_in, kd_in, dx_ref, pd_ref, kd_ref, sd_ref):
    dx_ref[...] = dx_in[...]
    pd_ref[...] = pd_in[...]
    kd_ref[...] = kd_in[0:27, :]
    for e in range(2):
        sd_ref[e] = kd_in[27 + e, 0]


def local(x, g, w, k, sharp):
    n_col, n_bulk = lax.axis_size("col"), lax.axis_size("bulk")
    scale = 1.0 / math.sqrt(x.shape[1] * x.shape[2] * x.shape[3] * n_col * n_bulk)
    place, flags = edge_tables()
    vmem = pl.BlockSpec(memory_space=pltpu.VMEM)
    smem = pl.BlockSpec(memory_space=pltpu.SMEM)
    hbm = pl.BlockSpec(memory_space=pl.ANY)
    rows1, rows2 = C // n_bulk, C3 // n_bulk

    def reduction(rows):
        return [
            pltpu.VMEM((n_bulk, rows, LANES), F32),
            pltpu.VMEM((n_bulk, rows, LANES), F32),
            pltpu.VMEM((n_col, rows, LANES), F32),
            pltpu.VMEM((n_bulk, rows, LANES), F32),
        ]

    def dma(count):
        return pltpu.SemaphoreType.DMA((count,))

    reduction_sems = [pltpu.SemaphoreType.DMA] * 6
    dx, pd, kd = pl.pallas_call(
        functools.partial(kernel, (n_col, n_bulk), scale),
        out_shape=(
            pltpu.VMEM((C, 4, 2, LANES), BF16),
            pltpu.VMEM((C3, C), F32),
            pltpu.VMEM((32, C3), F32),
        ),
        in_specs=[hbm, hbm, hbm, hbm, smem, hbm, vmem],
        out_specs=(vmem, vmem, vmem),
        scratch_shapes=[
            pltpu.VMEM(x.shape, BF16),
            pltpu.VMEM(g.shape, BF16),
            pltpu.VMEM(w.shape, BF16),
            pltpu.VMEM((27, C3), F32),
            pltpu.VMEM(place.shape, BF16),
            pltpu.SemaphoreType.DMA((5,)),
            pltpu.VMEM((2, 4, C, LANES), BF16),
            pltpu.VMEM((2, 4, C, LANES), BF16),
            pltpu.VMEM((4, 4, C, LANES), BF16),
            pltpu.VMEM((2, 4, C, LANES), BF16),
            pltpu.VMEM((2, 32, LANES), BF16),
            pltpu.VMEM((2, 9, 32, LANES), BF16),
            pltpu.VMEM((4, LANES, LANES), BF16),
            pltpu.VMEM((LANES, LANES), BF16),
            pltpu.VMEM((LANES, LANES), BF16),
            pltpu.VMEM((LANES, 3 * LANES), F32),
            pltpu.VMEM((3 * LANES, LANES), F32),
            pltpu.VMEM((27, C3, LANES), F32),
            pltpu.VMEM((3, 6, 4, C3, LANES), F32),
            pltpu.VMEM((3, C3, LANES), F32),
            pltpu.VMEM((4, 4, C3, LANES), BF16),
            pltpu.VMEM((C3, LANES), BF16),
            pltpu.VMEM((3, 4, 4, C3, LANES), F32),
            pltpu.VMEM((C3, LANES), BF16),
            pltpu.VMEM((2, 4, C3, LANES), BF16),
            pltpu.VMEM((3, LANES, LANES), F32),
            pltpu.VMEM((2, 4, C3, LANES), F32),
            pltpu.VMEM((3, C, LANES), BF16),
            pltpu.VMEM((2, C, LANES), F32),
            pltpu.VMEM((C, LANES), F32),
            pltpu.VMEM((C3, LANES), F32),
        ]
        + reduction(rows1)
        + reduction(rows2)
        + [dma(6), dma(6), dma(18), dma(18)]
        + reduction_sems
        + reduction_sems,
        compiler_params=pltpu.CompilerParams(
            collective_id=0, has_side_effects=True, vmem_limit_bytes=56 * 2**20
        ),
    )(
        x,
        g,
        w,
        k.T,
        sharp,
        jnp.asarray(place, BF16),
        jnp.asarray(flags),
    )
    dx, pd, kd, sd = pl.pallas_call(
        hand_out,
        out_shape=(
            jax.ShapeDtypeStruct((C, 4, 2, LANES), BF16),
            jax.ShapeDtypeStruct((C3, C), F32),
            jax.ShapeDtypeStruct((27, C3), F32),
            jax.ShapeDtypeStruct((2,), F32),
        ),
        in_specs=[vmem, vmem, vmem],
        out_specs=(vmem, vmem, vmem, smem),
        compiler_params=pltpu.CompilerParams(vmem_limit_bytes=4 * 2**20),
    )(dx, pd, kd)
    return dx, pd, kd.T, sd


def solution(mesh):
    return jax.shard_map(
        local,
        mesh=mesh,
        in_specs=(P(None, None, "bulk", "col"), P(None, None, "bulk", "col"), P(), P(), P()),
        out_specs=(P(None, None, "bulk", "col"), P(), P(), P()),
        check_vma=False,
    )
```
